32 devices in a mesh: band: 8 (over z, y), sample: 4 (over x, core).
Axes of the slice: x: 2, y: 2, z: 4, core: 2. Of those that a mesh axis runs over, the one named last changes fastest.
Arguments:
- fields: bfloat16 [4, 69, 16, 512], P('sample', None, 'band'), may hold values from -6 to 6
- embed_w: bfloat16 [552, 1024], replicated, may hold values from -0.25 to 0.25
- embed_b: float32 [1024], replicated, may hold values from -3 to 3
- merge_ids: int32 [8, 256], P('band'), may hold values from 0 to 255, as said below
- ln_gain: float32 [1024], replicated, may hold values from 0.5 to 2
- w_up: bfloat16 [1024, 2048], replicated, may hold values from -0.1875 to 0.1875
- w_down: bfloat16 [2048, 1024], replicated, may hold values from -0.125 to 0.125
- d_out: bfloat16 [4, 1408, 1024], P('sample', 'band'), may hold values from -6 to 6
Outputs:
- mixed: bfloat16 [4, 1408, 1024], P('sample', 'band')
- grad_w: float32 [552, 1024], replicated
- grad_b: float32 [1024], replicated
The draws below stay inside these ranges and needn't reach their ends.
Inputs may be any that keep to these rules, and one draw needn't show every extreme that they name: `merge_ids`: in row b, with f = 4 in the 1 row at each end, 2 in the next 1 row at each end and 1 elsewhere, the ids run from 0 to 256 / f - 1 without falling and without gaps, each naming 1 to 2 f - 1 consecutive patches, and some naming exactly 2 f - 1.
All inputs are finite; a program needn't handle non-finite values.
Results may differ from the reference program's by a relative error of at most 0.009.
Values may be sent and summed in bfloat16 or wider, within the bound.
A program may use at most 64 MiB of HBM per device.

```python
import math
import jax
import jax.numpy as jnp
from jax import lax

V = 69
D = 1024
FF = 2048
P_SIZE = 2
LONP = 256
BANDS = 8
SAMPLES = 4
NLAT = 16
NLON = 512
K = 552
MT = 176
MERGED = 1408


def draw_merge_ids(key, part):
    rows = jnp.arange(BANDS, dtype=jnp.int32)
    distance = jnp.minimum(rows, BANDS - 1 - rows)
    factor = jnp.where(distance < BANDS // 8, 4, jnp.where(distance < BANDS // 4, 2, 1)).astype(jnp.int32)
    pair_len = 2 * factor
    raw_bits = jax.random.randint(key, (BANDS, LONP // 2), 0, 1048576, dtype=jnp.int32)
    first_len = 1 + raw_bits % (pair_len[:, None] - 1)
    column = jnp.arange(LONP // 2, dtype=jnp.int32)[None, :]
    first_len = jnp.where(column == 0, pair_len[:, None] - 1, first_len)
    position = jnp.arange(LONP, dtype=jnp.int32)[None, :]
    pair_id = position // pair_len[:, None]
    pair_offset = position % pair_len[:, None]
    first_here = jnp.take_along_axis(first_len, pair_id, axis=1)
    return (2 * pair_id + (pair_offset >= first_here).astype(jnp.int32)).astype(jnp.int32)


def shard_levels(key, shape, shards, low, top_value):
    gain, own = 1.0, jax.random.fold_in(key, 6)
    for dim, parts in shards:
        steps = jnp.exp(jax.random.uniform(jax.random.fold_in(own, dim), (parts,), jnp.float32, low / len(shards), top_value / len(shards)))
        gain = gain * jnp.repeat(steps, shape[dim] // parts).reshape([-1 if axis == dim else 1 for axis in range(len(shape))])
    return gain


def noise(key, dims, width, reach, cuts=(), kind=jnp.bfloat16):
    gain = shard_levels(key, dims, cuts, -0.22, 0.18) if cuts else 1.0
    entries = jax.random.normal(key, dims, jnp.float32) * width * gain
    return jnp.minimum(jnp.maximum(entries, -reach), reach).astype(kind)


def setup_inputs(seed: int = 0) -> dict:
    splits = jax.random.split(jax.random.key(seed), 9)
    return {
        "fields": noise(splits[0], (SAMPLES, V, NLAT, NLON), 1.0, 6.0, ((0, 4), (2, 8))),
        "embed_w": noise(splits[1], (K, D), K ** -0.5, 0.25),
        "embed_b": noise(splits[2], (D,), 0.5, 3.0, (), jnp.float32),
        "merge_ids": draw_merge_ids(jax.random.fold_in(splits[8], 71), 0),
        "ln_gain": jnp.clip(jnp.exp(jax.random.uniform(splits[4], (D,), jnp.float32, math.log(0.5), math.log(2.0))), 0.5, 2.0),
        "w_up": noise(splits[5], (D, FF), D ** -0.5, 0.1875),
        "w_down": noise(splits[6], (FF, D), FF ** -0.5, 0.125),
        "d_out": noise(splits[7], (SAMPLES, MERGED, D), 1.0, 6.0, ((0, 4), (1, 8))),
    }


def band_layout(band_total, lon_patches):
    counts = []
    for b in range(band_total):
        distance = min(b, band_total - 1 - b)
        factor = 4 if distance < band_total // 8 else 2 if distance < band_total // 4 else 1
        counts.append(lon_patches // factor)
    starts = [0]
    for c in counts:
        starts.append(starts[-1] + c)
    return (counts, starts)

def ffn_block(tokens, ln_gain, w_up, w_down):
    widened = tokens.astype(jnp.float32)
    centred = widened - lax.optimization_barrier(jnp.mean(widened, axis=-1, keepdims=True))
    variance = lax.optimization_barrier(jnp.mean(centred * centred, axis=-1, keepdims=True))
    normed = (centred * lax.rsqrt(variance + 1e-05) * ln_gain).astype(jnp.bfloat16)
    hidden_pre = jnp.dot(normed, w_up, preferred_element_type=jnp.float32)
    hidden = jax.nn.gelu(hidden_pre, approximate=True).astype(jnp.bfloat16)
    return (widened + jnp.dot(hidden, w_down, preferred_element_type=jnp.float32)).astype(jnp.bfloat16)

def reference(fields, embed_w, embed_b, merge_ids, ln_gain, w_up, w_down, d_out):
    counts, starts = band_layout(BANDS, LONP)
    rotate = MT - LONP // 8
    slot_iota = jnp.arange(LONP, dtype=jnp.int32)
    onehot = (merge_ids[:, None, :] == slot_iota[None, :, None]).astype(jnp.float32)
    members = lax.optimization_barrier(jnp.sum(onehot, axis=2, keepdims=True))
    safe_count = jnp.where(members > 0, members, 1.0)
    grad_total = jnp.zeros((K + 1, D), jnp.float32)
    outputs = []
    for s in range(SAMPLES):
        padded = jnp.pad(fields[s], ((0, 0), (1, 1), (0, 0)))
        stacked = jnp.stack([padded[:, r:r + P_SIZE * BANDS:P_SIZE, :] for r in range(P_SIZE + 2)], axis=1)
        patches = stacked.reshape(V, P_SIZE + 2, BANDS, LONP, P_SIZE).transpose(2, 3, 0, 1, 4).reshape(BANDS, LONP, K)
        embedded = (jnp.einsum('btk,kd->btd', patches.astype(jnp.float32), embed_w.astype(jnp.float32)) + embed_b).astype(jnp.bfloat16)
        merged = (jnp.einsum('bmt,btd->bmd', onehot, embedded.astype(jnp.float32)) / safe_count).astype(jnp.bfloat16)
        mean_patch = (jnp.einsum('bmt,btk->bmk', onehot, patches.astype(jnp.float32)) / safe_count).astype(jnp.bfloat16)
        tokens = jnp.concatenate([merged[b, :counts[b]] for b in range(BANDS)], axis=0)
        patch_rows = jnp.concatenate([mean_patch[b, :counts[b]] for b in range(BANDS)], axis=0)
        tokens = jnp.roll(tokens, rotate, axis=0)
        patch_rows = jnp.roll(patch_rows, rotate, axis=0)

        def block_of(inputs):
            return ffn_block(inputs, ln_gain, w_up, w_down)
        mixed, pullback = jax.vjp(block_of, tokens)
        grad_tokens = pullback(d_out[s])[0]
        weight_part = jnp.dot(patch_rows.T, grad_tokens, preferred_element_type=jnp.float32)
        bias_part = lax.optimization_barrier(jnp.sum(grad_tokens.astype(jnp.float32), axis=0))
        grad_total = grad_total + jnp.concatenate([weight_part, bias_part[None, :]], axis=0)
        outputs.append(mixed)
    scale = 1.0 / math.sqrt(SAMPLES * MERGED)
    return (jnp.stack(outputs), grad_total[:K] * scale, grad_total[K] * scale)
```

```python
import functools
import math

import jax
import jax.numpy as jnp
from jax import lax
from jax.experimental import pallas as pl
from jax.experimental.pallas import tpu as pltpu
from jax.sharding import PartitionSpec as P

MESH = pl.DeviceIdType.MESH


def round_up(value, step):
    return -(-value // step) * step


def band_layout(band_total, lon_patches):
    counts = []
    for b in range(band_total):
        distance = min(b, band_total - 1 - b)
        factor = 4 if distance < band_total // 8 else 2 if distance < band_total // 4 else 1
        counts.append(lon_patches // factor)
    starts = [0]
    for c in counts:
        starts.append(starts[-1] + c)
    return (counts, starts)


def emit(mixed_hbm, grad_ref, bias_ref, mixed_out, w_out, b_out, staged, b_staged, sems):
    keep = pltpu.make_async_copy(mixed_hbm, mixed_out, sems.at[0])
    keep.start()
    features = w_out.shape[0]
    b_staged[...] = bias_ref[...]
    copies = [keep, pltpu.make_async_copy(b_staged, b_out, sems.at[1])]
    copies[1].start()
    step = 144
    for i, low in enumerate(range(0, features, step)):
        span = pl.ds(low, min(step, features - low))
        staged[span, :] = grad_ref[span, :].astype(jnp.float32)
        copy = pltpu.make_async_copy(staged.at[span], w_out.at[span], sems.at[2 + i])
        copy.start()
        copies.append(copy)
    for copy in copies:
        copy.wait()


def kernel(
    counts, rotate, shard_rows, features, granule, samples, scale,
    own_hbm, ids_hbm, bias_hbm, gain_hbm, embed_hbm, up_hbm, down_hbm, cot_hbm,
    mixed_ref, w_ref, b_ref,
    own_ref, ids_ref, bias_ref, gain_ref,
    embed, up, down, cot, grid, packed, rows_all, normed, grads, grads_in,
    band_out, band_in, total_w, final,
    load, halo_send, halo_recv, row_send, row_recv,
    rows_send, rows_forward, rows_done, grads_send, grads_recv,
    band_send, band_recv, gather_send, gather_chip_send, gather_core_send, gather_recv,
    d_hid, hid, held_tokens,
):
    bands = total = len(counts)
    band, sample = lax.axis_index("band"), lax.axis_index("sample")
    chips = samples // 2
    chip, core = lax.div(sample, 2), lax.rem(sample, 2)
    other = 1 - core
    partner = (band, 2 * chip + other)
    chip_of = [lax.rem(chip + o, chips) for o in range(1, chips)]
    band_offsets = sorted(range(1, bands), key=lambda o: (min(o, bands - o), o))
    band_of = [lax.rem(band + o, bands) for o in band_offsets]
    peers = [2 * x + core for x in chip_of] + [2 * x + other for x in chip_of]
    peers = peers + [2 * chip + other]

    greeted = [(band, s) for s in peers] + [(b, sample) for b in band_of]
    barrier = pltpu.get_barrier_semaphore()
    for peer in greeted:
        pl.semaphore_signal(barrier, inc=1, device_id=peer, device_id_type=MESH)

    loads = [
        pltpu.make_async_copy(src, dst, load.at[i])
        for i, (src, dst) in enumerate(
            (
                (embed_hbm, embed), (up_hbm, up), (down_hbm, down), (cot_hbm, cot),
                (own_hbm, own_ref), (ids_hbm, ids_ref), (bias_hbm, bias_ref), (gain_hbm, gain_ref),
            )
        )
    ]
    for i in (4, 5, 3, 2, 0, 6, 7, 1):
        loads[i].start()
    def remote(src, dst, send, recv, device):
        return pltpu.make_async_remote_copy(
            src_ref=src, dst_ref=dst, send_sem=send, recv_sem=recv,
            device_id=device, device_id_type=MESH,
        )

    pad_v = grid.shape[0] // 4
    landed = rows_all.at[sample]
    up_halo = remote(
        grid.at[pl.ds(pad_v, pad_v)], grid.at[pl.ds(3 * pad_v, pad_v)],
        halo_send.at[0], halo_recv.at[0], (lax.rem(band + total - 1, total), sample),
    )
    down_halo = remote(
        grid.at[pl.ds(2 * pad_v, pad_v)], grid.at[pl.ds(0, pad_v)],
        halo_send.at[1], halo_recv.at[1], (lax.rem(band + 1, total), sample),
    )
    is_first, is_last = band == 0, band == total - 1
    not_first, not_last = band > 0, band < total - 1
    channels = own_ref.shape[0]
    loads[4].wait()
    grid[pl.ds(pad_v, 2 * pad_v), :] = jnp.zeros((2 * pad_v, grid.shape[1]), grid.dtype)
    for line in range(2):
        grid[pl.ds((1 + line) * pad_v, channels), :] = own_ref[:, line, :]
    lon, cells, width = packed.shape[0], grid.shape[1], packed.shape[1]
    slot = lax.broadcasted_iota(jnp.int32, (lon, lon), 0)
    loads[5].wait()
    onehot = (ids_ref[...] == slot).astype(jnp.float32)
    members = jnp.sum(onehot, axis=1, keepdims=True)
    safe = jnp.where(members > 0, members, 1.0)
    onehot = onehot.astype(jnp.bfloat16)
    patch = lax.broadcasted_iota(jnp.int32, (lon, cells), 0)
    cell = lax.broadcasted_iota(jnp.int32, (lon, cells), 1)
    picks = [
        jnp.dot(
            onehot, (cell == 2 * patch + q).astype(jnp.float32).astype(jnp.bfloat16),
            preferred_element_type=jnp.float32,
        ).astype(jnp.bfloat16)
        for q in range(2)
    ]
    rows = lax.broadcasted_iota(jnp.int32, (4 * pad_v, width), 0)
    column = lax.broadcasted_iota(jnp.int32, (4 * pad_v, width), 1)
    r = (
        (rows >= pad_v).astype(jnp.int32)
        + (rows >= 2 * pad_v).astype(jnp.int32)
        + (rows >= 3 * pad_v).astype(jnp.int32)
    )
    place = 8 * (rows - pad_v * r) + 2 * r
    moves = [(column == place + q).astype(jnp.float32).astype(jnp.bfloat16) for q in range(2)]
    pl.semaphore_wait(barrier, len(greeted))
    pl.when(not_first)(up_halo.start)
    pl.when(not_last)(down_halo.start)

    @pl.when(is_first)
    def _():
        grid[pl.ds(0, pad_v), :] = jnp.zeros((pad_v, grid.shape[1]), grid.dtype)

    @pl.when(is_last)
    def _():
        grid[pl.ds(3 * pad_v, pad_v), :] = jnp.zeros((pad_v, grid.shape[1]), grid.dtype)

    pl.when(not_last)(up_halo.wait_recv)
    pl.when(not_first)(down_halo.wait_recv)
    ordered = None
    for q in range(2):
        summed = lax.dot_general(
            picks[q], grid[...], (((1,), (1,)), ((), ())), preferred_element_type=jnp.float32
        )
        mean = (summed / safe).astype(jnp.bfloat16)
        part = jnp.dot(mean, moves[q], preferred_element_type=jnp.float32)
        ordered = part if ordered is None else ordered + part
    ones = lax.broadcasted_iota(jnp.int32, (lon, width), 1) == features
    packed[...] = jnp.where(ones, 1.0, ordered).astype(packed.dtype)

    my_count = sum(jnp.where(band == b, c, 0) for b, c in enumerate(counts))
    my_start = rotate + sum(jnp.where(band > b, c, 0) for b, c in enumerate(counts))
    row_copies = []
    for i in range(lon // granule):
        unwrapped = my_start + granule * i
        target = lax.rem(lax.div(unwrapped, shard_rows), total)
        offset = pl.multiple_of(lax.rem(unwrapped, shard_rows), granule)
        valid = granule * i < my_count
        here = target == band
        src, dst = packed.at[pl.ds(granule * i, granule)], landed.at[pl.ds(offset, granule)]
        copy = remote(src, dst, row_send.at[i], row_recv, (target, sample))
        keep = pltpu.make_async_copy(src, dst, row_recv)
        away = jnp.logical_and(valid, jnp.logical_not(here))
        pl.when(away)(copy.start)
        pl.when(jnp.logical_and(valid, here))(keep.start)
        row_copies.append((away, copy))
    for i in (2, 3):
        loads[i].wait()
    hidden_width = up.shape[1]
    tile = 512
    across = (((1,), (1,)), ((), ()))
    for t in range(hidden_width // tile):
        span = slice(t * tile, (t + 1) * tile)
        d_hid[:, span] = lax.dot_general(
            cot[...], down[span, :], across, preferred_element_type=jnp.float32
        ).astype(jnp.bfloat16)
    pltpu.make_async_copy(landed, landed, row_recv).wait()

    sends = []

    def send_rows(s, send, device):
        copy = remote(rows_all.at[s], rows_all.at[s], send, rows_done.at[s], device)
        copy.start()
        sends.append(copy)

    def rows_arrive(s):
        pltpu.make_async_copy(rows_all.at[s], rows_all.at[s], rows_done.at[s]).wait()

    for i, x in enumerate(chip_of):
        send_rows(sample, rows_send.at[i], (band, 2 * x + core))
    send_rows(sample, rows_send.at[chips - 1], partner)

    for i in (0, 6, 7):
        loads[i].wait()
    tokens = (
        jnp.dot(landed[:, :features], embed[...], preferred_element_type=jnp.float32)
        + bias_ref[...]
    ).astype(jnp.bfloat16).astype(jnp.float32)
    model_width = tokens.shape[1]
    centred = tokens - jnp.mean(tokens, axis=-1, keepdims=True)
    inverse = lax.rsqrt(jnp.mean(centred * centred, axis=-1, keepdims=True) + 1e-05)
    normed[...] = (centred * inverse * gain_ref[...]).astype(jnp.bfloat16)
    held_tokens[...] = tokens
    d_normed = jnp.zeros_like(tokens)
    loads[1].wait()
    slope = math.sqrt(2.0 / math.pi)
    for t in range(hidden_width // tile):
        span = slice(t * tile, (t + 1) * tile)
        pre = jnp.dot(normed[...], up[:, span], preferred_element_type=jnp.float32)
        d_hidden = d_hid[:, span].astype(jnp.float32)
        square = pre * pre
        bent = jnp.tanh(slope * (pre + 0.044715 * (square * pre)))
        cdf = 0.5 * (1.0 + bent)
        hid[:, span] = (pre * cdf).astype(jnp.bfloat16)
        steep = cdf + (0.5 * slope) * pre * (1.0 - bent * bent) * (
            1.0 + (3.0 * 0.044715) * square
        )
        d_pre = (d_hidden * steep).astype(jnp.bfloat16)
        d_normed = d_normed + lax.dot_general(
            d_pre, up[:, span], across, preferred_element_type=jnp.float32
        )
    d_scaled = d_normed.astype(jnp.bfloat16).astype(jnp.float32) * gain_ref[...]
    d_var = jnp.sum(d_scaled * centred, axis=-1, keepdims=True) * (
        -0.5 * inverse * inverse * inverse
    )
    d_centred = d_scaled * inverse + centred * (d_var * (2.0 / model_width))
    d_tokens = d_centred - jnp.mean(d_centred, axis=-1, keepdims=True)
    grad = (cot[...].astype(jnp.float32) + d_tokens).astype(jnp.bfloat16)
    columns = grads.shape[2]
    for s in range(samples):
        grads[s] = grad[:, s * columns : (s + 1) * columns]

    grad_copies = []
    for i, s in enumerate(peers):
        copy = remote(
            grads.at[s], grads_in.at[i], grads_send.at[i], grads_recv.at[i], (band, s)
        )
        copy.start()
        grad_copies.append(copy)
    mixed = held_tokens[...]
    for t in range(hidden_width // tile):
        span = slice(t * tile, (t + 1) * tile)
        mixed = mixed + jnp.dot(hid[:, span], down[span, :], preferred_element_type=jnp.float32)
    mixed_ref[...] = mixed.astype(jnp.bfloat16)
    for i, x in enumerate(chip_of):
        rows_arrive(2 * x + core)
        send_rows(2 * x + core, rows_forward.at[i], partner)
    part_rows = total_w.shape[1]
    span_rows = bands * part_rows

    def product(s, values):
        full = lax.dot_general(
            rows_all[s], values, (((0,), (0,)), ((), ())), preferred_element_type=jnp.float32
        )
        return full[:span_rows].reshape(bands, part_rows, columns)

    total_w[...] = product(sample, grads[sample])
    arrivals = [len(peers) - 1] + list(range(len(peers) - 1))
    for i in arrivals:
        grad_copies[i].wait_recv()
        if i == len(peers) - 1:
            source = 2 * chip + other
        else:
            back = lax.rem(chip + chips - 1 - i % (chips - 1), chips)
            source = 2 * back + (core if i < chips - 1 else other)
        if i >= chips - 1:
            rows_arrive(source)
        total_w[...] += product(source, grads_in[i])
    held = total_w[...]
    band_out[...] = held.astype(jnp.bfloat16)
    band_copies = []
    for i, b in enumerate(band_of):
        copy = remote(
            band_out.at[b], band_in.at[i], band_send.at[i], band_recv.at[i], (b, sample)
        )
        copy.start()
        band_copies.append(copy)
    result = total_w[band]
    for i, copy in enumerate(band_copies):
        copy.wait_recv()
        result = result + band_in[i].astype(jnp.float32)
    final[sample, band] = (result * scale).astype(jnp.bfloat16)
    sends += grad_copies + band_copies

    def piece(s, b):
        return final.at[s, b]

    def spread(s, b, i, j, chips_too):
        if chips_too:
            for c, x in enumerate(chip_of):
                copy = remote(
                    piece(s, b), piece(s, b), gather_chip_send.at[c, j],
                    gather_recv.at[s, b], (band, 2 * x + core),
                )
                copy.start()
                sends.append(copy)
        copy = remote(
            piece(s, b), piece(s, b), gather_core_send.at[i, j], gather_recv.at[s, b], partner
        )
        copy.start()
        sends.append(copy)

    def arrive(s, b):
        pltpu.make_async_copy(piece(s, b), piece(s, b), gather_recv.at[s, b]).wait()

    for j, b in enumerate(band_of):
        copy = remote(
            piece(sample, band), piece(sample, band), gather_send.at[j],
            gather_recv.at[sample, band], (b, sample),
        )
        copy.start()
        sends.append(copy)
    spread(sample, band, 0, bands - 1, True)
    for j, b in enumerate(band_of):
        arrive(sample, b)
        spread(sample, b, 0, j, True)
    for i, x in enumerate(chip_of):
        for j, b in enumerate([band] + band_of):
            arrive(2 * x + core, b)
            spread(2 * x + core, b, i + 1, j, False)
    for x in chip_of + [chip]:
        for b in [band] + band_of:
            arrive(2 * x + other, b)
    for s in range(samples):
        span = slice(s * columns, (s + 1) * columns)
        for b in range(bands):
            w_ref[b * part_rows : (b + 1) * part_rows, span] = final[s, b]
        b, line = divmod(features, part_rows)
        b_ref[:, span] = final[s, b].astype(jnp.float32)[line : line + 1]
    for copy in sends:
        copy.wait_send()
    for away, copy in row_copies:
        pl.when(away)(copy.wait_send)
    pl.when(not_first)(up_halo.wait_send)
    pl.when(not_last)(down_halo.wait_send)


def body(fields, embed_w, embed_b, merge_ids, ln_gain, w_up, w_down, d_out):
    bands = lax.axis_size("band")
    samples = lax.axis_size("sample")
    lon = merge_ids.shape[1]
    counts, starts = band_layout(bands, lon)
    shard_rows = starts[-1] // bands
    rotate = shard_rows - lon // 8
    granule = functools.reduce(math.gcd, counts + [rotate, shard_rows])
    features, model_width = embed_w.shape
    channels, lat_rows, cells = fields.shape[1:]
    pad_v = round_up(channels, 16)
    part_rows = round_up(-(-(features + 1) // bands), 8)
    width = round_up(bands * part_rows, 128)
    vmem = pl.BlockSpec(memory_space=pltpu.VMEM)
    dma = pltpu.SemaphoreType.DMA

    scale = 1.0 / math.sqrt(samples * starts[-1])
    chips, columns = samples // 2, model_width // samples
    hidden_width = w_up.shape[1]
    piece = (bands, part_rows, columns)
    far = max(chips - 1, 1)
    bf16 = jnp.bfloat16
    hbm = pl.BlockSpec(memory_space=pl.ANY)
    f32 = jnp.float32
    mixed, grad, grad_b = pl.pallas_call(
        functools.partial(
            kernel, counts, rotate, shard_rows, features, granule, samples, scale
        ),
        out_shape=(
            pltpu.VMEM((shard_rows, model_width), bf16),
            pltpu.VMEM((bands * part_rows, model_width), bf16),
            pltpu.VMEM((1, model_width), jnp.float32),
        ),
        in_specs=[pl.BlockSpec(memory_space=pltpu.HBM)] * 8,
        out_specs=(vmem, vmem, vmem),
        scratch_shapes=[
            pltpu.VMEM(fields.shape[1:], bf16),
            pltpu.VMEM(merge_ids.shape, jnp.int32),
            pltpu.VMEM((1, model_width), f32),
            pltpu.VMEM((1, model_width), f32),
            pltpu.VMEM(embed_w.shape, bf16),
            pltpu.VMEM(w_up.shape, bf16),
            pltpu.VMEM(w_down.shape, bf16),
            pltpu.VMEM((shard_rows, model_width), bf16),
            pltpu.VMEM((4 * pad_v, cells), bf16),
            pltpu.VMEM((lon, width), bf16),
            pltpu.VMEM((samples, shard_rows, width), bf16),
            pltpu.VMEM((shard_rows, model_width), bf16),
            pltpu.VMEM((samples, shard_rows, columns), bf16),
            pltpu.VMEM((samples - 1, shard_rows, columns), bf16),
            pltpu.VMEM(piece, bf16),
            pltpu.VMEM((bands - 1,) + piece[1:], bf16),
            pltpu.VMEM(piece, jnp.float32),
            pltpu.VMEM((samples,) + piece, bf16),
            dma((8,)),
            dma((2,)),
            dma((2,)),
            dma((lon // granule,)),
            dma(()),
            dma((chips,)),
            dma((far,)),
            dma((samples,)),
            dma((samples - 1,)),
            dma((samples - 1,)),
            dma((bands - 1,)),
            dma((bands - 1,)),
            dma((bands - 1,)),
            dma((far, bands)),
            dma((chips, bands)),
            dma((samples, bands)),
            pltpu.VMEM((shard_rows, hidden_width), bf16),
            pltpu.VMEM((shard_rows, hidden_width), bf16),
            pltpu.VMEM((shard_rows, model_width), jnp.float32),
        ],
        compiler_params=pltpu.CompilerParams(
            collective_id=0, has_side_effects=True, vmem_limit_bytes=32 << 20
        ),
    )(*[
        pltpu.with_memory_space_constraint(x, pltpu.HBM)
        for x in (
            fields[0], merge_ids, embed_b[None], ln_gain[None], embed_w, w_up, w_down, d_out[0]
        )
    ])
    mixed, grad, grad_b = pl.pallas_call(
        emit,
        out_shape=(
            jax.ShapeDtypeStruct((shard_rows, model_width), bf16),
            jax.ShapeDtypeStruct((features, model_width), f32),
            jax.ShapeDtypeStruct((1, model_width), f32),
        ),
        in_specs=[vmem, vmem, vmem],
        out_specs=(hbm, hbm, hbm),
        scratch_shapes=[
            pltpu.VMEM((features, model_width), f32),
            pltpu.VMEM((1, model_width), f32),
            dma((2 + -(-features // 144),)),
        ],
        compiler_params=pltpu.CompilerParams(vmem_limit_bytes=16 << 20),
    )(mixed, grad, grad_b)
    return mixed[None], grad, grad_b[0]


def solution(mesh):
    return jax.shard_map(
        body,
        mesh=mesh,
        in_specs=(
            P("sample", None, "band", None),
            P(),
            P(),
            P("band", None),
            P(),
            P(),
            P(),
            P("sample", "band", None),
        ),
        out_specs=(P("sample", "band", None), P(), P()),
        check_vma=False,
    )
```

```python
import functools
import math

import jax
import jax.numpy as jnp
from jax import lax
from jax.experimental import pallas as pl
from jax.experimental.pallas import tpu as pltpu
from jax.sharding import PartitionSpec as P

MESH = pl.DeviceIdType.MESH


def round_up(value, step):
    return -(-value // step) * step


def band_layout(band_total, lon_patches):
    counts = []
    for b in range(band_total):
        distance = min(b, band_total - 1 - b)
        factor = 4 if distance < band_total // 8 else 2 if distance < band_total // 4 else 1
        counts.append(lon_patches // factor)
    starts = [0]
    for c in counts:
        starts.append(starts[-1] + c)
    return (counts, starts)


def flip(value, mask):
    for bit in range(mask.bit_length()):
        if mask >> bit & 1:
            value = value + (1 - 2 * lax.rem(lax.div(value, 1 << bit), 2)) * (1 << bit)
    return value


def emit(inner, mixed_ref, final_ref, mixed_out, w_out, b_out, staged, b_staged, sems):
    members, lines, part_rows, columns = final_ref.shape
    blocks = members // inner
    features = w_out.shape[0]
    copies = [pltpu.make_async_copy(mixed_ref, mixed_out, sems.at[0])]
    copies[0].start()
    for line in range(lines):
        start = line * inner * part_rows
        for pair in range(inner):
            low = start + pair * part_rows
            rows = min(part_rows, features - low)
            for m in range(blocks):
                values = final_ref[pair * blocks + m, line].astype(jnp.float32)
                if rows > 0:
                    staged[low : low + rows, m * columns : (m + 1) * columns] = values[:rows]
                if low <= features < low + part_rows:
                    b_staged[:, m * columns : (m + 1) * columns] = values[
                        features - low : features - low + 1
                    ]
        rows = min(inner * part_rows, features - start)
        if rows > 0:
            span = pl.ds(start, rows)
            copy = pltpu.make_async_copy(staged.at[span], w_out.at[span], sems.at[2 + line])
            copy.start()
            copies.append(copy)
    copies.append(pltpu.make_async_copy(b_staged, b_out, sems.at[1]))
    copies[-1].start()
    for copy in copies:
        copy.wait()


def kernel(
    counts, rotate, shard_rows, features, granule, samples, inner, scale,
    own_hbm, ids_hbm, bias_hbm, gain_hbm, embed_hbm, up_hbm, down_hbm, cot_hbm,
    mixed_ref, final,
    own_ref, ids_ref, bias_ref, gain_ref,
    embed, up, down, cot, grid, packed, rows_all, normed, grads, grads_in,
    band_out, band_in, total_w,
    load, halo_send, halo_recv, row_send, row_recv,
    rows_send, rows_forward, rows_done, grads_send, grads_recv,
    band_send, band_recv, along_send, across_send, forward_send, gather_recv,
    d_hid, hid, held_tokens,
):
    total = len(counts)
    lines, chips = total // inner, samples // 2
    band, sample = lax.axis_index("band"), lax.axis_index("sample")
    line, pair = lax.div(band, inner), lax.rem(band, inner)
    chip, core = lax.div(sample, 2), lax.rem(sample, 2)
    half = lax.div(line, lines // 2)
    other = 1 - core
    partner = (band, 2 * chip + other)

    def near(step, turn):
        p, c = step
        return (lax.rem(pair + p, inner), lax.rem(chip + c, chips), core if turn == 0 else other)

    def behind(step, turn):
        p, c = step
        return (
            lax.rem(pair + inner - p, inner),
            lax.rem(chip + chips - c, chips),
            core if turn == 0 else other,
        )

    def device(spot):
        p, c, k = spot
        return (line * inner + p, 2 * c + k)

    def block(spot):
        p, c, k = spot
        return 2 * c + lax.rem(k + half, 2)

    def member(spot):
        return spot[0] * samples + block(spot)

    steps = [(p, c) for p in range(inner) for c in range(chips)]
    away_steps = sorted(steps[1:], key=lambda step: (step[0] > 0) + (step[1] > 0))
    here_spot = (pair, chip, core)
    my_block, mine = block(here_spot), member(here_spot)
    side_steps = [step for step in away_steps if step[0] == 0]
    peer_keys = [((0, 0), 1)] + [(step, turn) for step in side_steps for turn in (1, 0)]
    masks = sorted(range(1, lines), reverse=True)

    def along(mask, p):
        return (flip(line, mask) * inner + p, 2 * chip + (other if 2 * mask >= lines else core))

    shifts = [(mask, p) for mask in masks for p in reversed(range(inner))]
    shifts += [(0, p) for p in range(1, inner)]

    def turned(p):
        return lax.rem(pair + p, inner)

    greeted = [device(near(step, turn)) for step in away_steps for turn in (0, 1)] + [partner]
    greeted += [(flip(line, m) * inner + p, sample) for m in masks for p in range(inner)]
    greeted += [along(m, p) for m in masks if 2 * m >= lines for p in range(inner)]
    barrier = pltpu.get_barrier_semaphore()
    for peer in greeted:
        pl.semaphore_signal(barrier, inc=1, device_id=peer, device_id_type=MESH)

    loads = [
        pltpu.make_async_copy(src, dst, load.at[i])
        for i, (src, dst) in enumerate(
            (
                (embed_hbm, embed), (up_hbm, up), (down_hbm, down), (cot_hbm, cot),
                (own_hbm, own_ref), (ids_hbm, ids_ref), (bias_hbm, bias_ref), (gain_hbm, gain_ref),
            )
        )
    ]
    for i in (4, 5, 3, 2, 0, 6, 7, 1):
        loads[i].start()
    def remote(src, dst, send, recv, device):
        return pltpu.make_async_remote_copy(
            src_ref=src, dst_ref=dst, send_sem=send, recv_sem=recv,
            device_id=device, device_id_type=MESH,
        )

    pad_v = grid.shape[0] // 4
    landed = rows_all.at[sample]
    up_halo = remote(
        grid.at[pl.ds(pad_v, pad_v)], grid.at[pl.ds(3 * pad_v, pad_v)],
        halo_send.at[0], halo_recv.at[0], (lax.rem(band + total - 1, total), sample),
    )
    down_halo = remote(
        grid.at[pl.ds(2 * pad_v, pad_v)], grid.at[pl.ds(0, pad_v)],
        halo_send.at[1], halo_recv.at[1], (lax.rem(band + 1, total), sample),
    )
    is_first, is_last = band == 0, band == total - 1
    not_first, not_last = band > 0, band < total - 1
    channels = own_ref.shape[0]
    loads[4].wait()
    grid[pl.ds(pad_v, 2 * pad_v), :] = jnp.zeros((2 * pad_v, grid.shape[1]), grid.dtype)
    for r in range(2):
        grid[pl.ds((1 + r) * pad_v, channels), :] = own_ref[:, r, :]
    lon, cells, width = packed.shape[0], grid.shape[1], packed.shape[1]
    slot = lax.broadcasted_iota(jnp.int32, (lon, lon), 0)
    loads[5].wait()
    onehot = (ids_ref[...] == slot).astype(jnp.float32)
    members = jnp.sum(onehot, axis=1, keepdims=True)
    safe = jnp.where(members > 0, members, 1.0)
    onehot = onehot.astype(jnp.bfloat16)
    patch = lax.broadcasted_iota(jnp.int32, (lon, cells), 0)
    cell = lax.broadcasted_iota(jnp.int32, (lon, cells), 1)
    picks = [
        jnp.dot(
            onehot, (cell == 2 * patch + q).astype(jnp.float32).astype(jnp.bfloat16),
            preferred_element_type=jnp.float32,
        ).astype(jnp.bfloat16)
        for q in range(2)
    ]
    rows = lax.broadcasted_iota(jnp.int32, (4 * pad_v, width), 0)
    column = lax.broadcasted_iota(jnp.int32, (4 * pad_v, width), 1)
    r = (
        (rows >= pad_v).astype(jnp.int32)
        + (rows >= 2 * pad_v).astype(jnp.int32)
        + (rows >= 3 * pad_v).astype(jnp.int32)
    )
    place = 8 * (rows - pad_v * r) + 2 * r
    moves = [(column == place + q).astype(jnp.float32).astype(jnp.bfloat16) for q in range(2)]
    pl.semaphore_wait(barrier, len(greeted))
    pl.when(not_first)(up_halo.start)
    pl.when(not_last)(down_halo.start)

    @pl.when(is_first)
    def _():
        grid[pl.ds(0, pad_v), :] = jnp.zeros((pad_v, grid.shape[1]), grid.dtype)

    @pl.when(is_last)
    def _():
        grid[pl.ds(3 * pad_v, pad_v), :] = jnp.zeros((pad_v, grid.shape[1]), grid.dtype)

    pl.when(not_last)(up_halo.wait_recv)
    pl.when(not_first)(down_halo.wait_recv)
    ordered = None
    for q in range(2):
        summed = lax.dot_general(
            picks[q], grid[...], (((1,), (1,)), ((), ())), preferred_element_type=jnp.float32
        )
        mean = (summed / safe).astype(jnp.bfloat16)
        part = jnp.dot(mean, moves[q], preferred_element_type=jnp.float32)
        ordered = part if ordered is None else ordered + part
    ones = lax.broadcasted_iota(jnp.int32, (lon, width), 1) == features
    packed[...] = jnp.where(ones, 1.0, ordered).astype(packed.dtype)

    my_count = sum(jnp.where(band == b, c, 0) for b, c in enumerate(counts))
    my_start = rotate + sum(jnp.where(band > b, c, 0) for b, c in enumerate(counts))
    row_copies = []
    for i in range(lon // granule):
        unwrapped = my_start + granule * i
        target = lax.rem(lax.div(unwrapped, shard_rows), total)
        offset = pl.multiple_of(lax.rem(unwrapped, shard_rows), granule)
        valid = granule * i < my_count
        here = target == band
        src, dst = packed.at[pl.ds(granule * i, granule)], landed.at[pl.ds(offset, granule)]
        copy = remote(src, dst, row_send.at[i], row_recv, (target, sample))
        keep = pltpu.make_async_copy(src, dst, row_recv)
        away = jnp.logical_and(valid, jnp.logical_not(here))
        pl.when(away)(copy.start)
        pl.when(jnp.logical_and(valid, here))(keep.start)
        row_copies.append((away, copy))
    for i in (2, 3):
        loads[i].wait()
    hidden_width = up.shape[1]
    tile = 512
    across = (((1,), (1,)), ((), ()))
    for t in range(hidden_width // tile):
        span = slice(t * tile, (t + 1) * tile)
        d_hid[:, span] = lax.dot_general(
            cot[...], down[span, :], across, preferred_element_type=jnp.float32
        ).astype(jnp.bfloat16)
    pltpu.make_async_copy(landed, landed, row_recv).wait()

    sends = []

    def send(src, dst, send_sem, recv_sem, target):
        copy = remote(src, dst, send_sem, recv_sem, target)
        copy.start()
        sends.append(copy)
        return copy

    def send_rows(m, send_sem, target):
        send(rows_all.at[m], rows_all.at[m], send_sem, rows_done.at[m], target)

    def rows_arrive(m):
        pltpu.make_async_copy(rows_all.at[m], rows_all.at[m], rows_done.at[m]).wait()

    for i, step in enumerate(side_steps):
        send_rows(sample, rows_send.at[i], device(near(step, 1)))
    send_rows(sample, rows_send.at[len(side_steps)], partner)

    for i in (0, 6, 7):
        loads[i].wait()
    tokens = (
        jnp.dot(landed[:, :features], embed[...], preferred_element_type=jnp.float32)
        + bias_ref[...]
    ).astype(jnp.bfloat16).astype(jnp.float32)
    model_width = tokens.shape[1]
    centred = tokens - jnp.mean(tokens, axis=-1, keepdims=True)
    inverse = lax.rsqrt(jnp.mean(centred * centred, axis=-1, keepdims=True) + 1e-05)
    normed[...] = (centred * inverse * gain_ref[...]).astype(jnp.bfloat16)
    held_tokens[...] = tokens
    d_normed = jnp.zeros_like(tokens)
    loads[1].wait()
    slope = math.sqrt(2.0 / math.pi)
    for t in range(hidden_width // tile):
        span = slice(t * tile, (t + 1) * tile)
        pre = jnp.dot(normed[...], up[:, span], preferred_element_type=jnp.float32)
        d_hidden = d_hid[:, span].astype(jnp.float32)
        square = pre * pre
        bent = jnp.tanh(slope * (pre + 0.044715 * (square * pre)))
        cdf = 0.5 * (1.0 + bent)
        hid[:, span] = (pre * cdf).astype(jnp.bfloat16)
        steep = cdf + (0.5 * slope) * pre * (1.0 - bent * bent) * (
            1.0 + (3.0 * 0.044715) * square
        )
        d_pre = (d_hidden * steep).astype(jnp.bfloat16)
        d_normed = d_normed + lax.dot_general(
            d_pre, up[:, span], across, preferred_element_type=jnp.float32
        )
    d_scaled = d_normed.astype(jnp.bfloat16).astype(jnp.float32) * gain_ref[...]
    d_var = jnp.sum(d_scaled * centred, axis=-1, keepdims=True) * (
        -0.5 * inverse * inverse * inverse
    )
    d_centred = d_scaled * inverse + centred * (d_var * (2.0 / model_width))
    d_tokens = d_centred - jnp.mean(d_centred, axis=-1, keepdims=True)
    grad = (cot[...].astype(jnp.float32) + d_tokens).astype(jnp.bfloat16)
    columns = grads.shape[2]
    for m in range(samples):
        grads[m] = grad[:, m * columns : (m + 1) * columns]

    grad_copies = {}
    for i, key in reversed(list(enumerate(peer_keys))):
        spot = near(*key)
        grad_copies[key] = send(
            grads.at[block(spot)], grads_in.at[i], grads_send.at[i], grads_recv.at[i],
            device(spot),
        )

    mixed = held_tokens[...]
    for t in range(hidden_width // tile):
        span = slice(t * tile, (t + 1) * tile)
        mixed = mixed + jnp.dot(hid[:, span], down[span, :], preferred_element_type=jnp.float32)
    mixed_ref[...] = mixed.astype(jnp.bfloat16)
    part_rows = total_w.shape[1]
    span_rows = total * part_rows

    def product(s, values):
        full = lax.dot_general(
            rows_all[s], values, (((0,), (0,)), ((), ())), preferred_element_type=jnp.float32
        )
        return full[:span_rows].reshape(total, part_rows, columns)

    def origin(key):
        return device(behind(*key))[1]

    def add_product(key):
        grad_copies[key].wait_recv()
        total_w[...] += product(origin(key), grads_in[peer_keys.index(key)])

    total_w[...] = product(sample, grads[my_block])
    rows_arrive(origin(((0, 0), 1)))
    add_product(((0, 0), 1))
    for i, step in enumerate(side_steps):
        source = origin((step, 1))
        rows_arrive(source)
        send_rows(source, rows_forward.at[i], partner)
        add_product((step, 1))
    for step in side_steps:
        rows_arrive(origin((step, 0)))
        add_product((step, 0))

    band_copies = []
    for i, (m, p) in enumerate(shifts):
        target = along(m, turned(p))
        band_out[target[0]] = total_w[target[0]].astype(jnp.bfloat16)
        band_copies.append(
            send(band_out.at[target[0]], band_in.at[i], band_send.at[i], band_recv.at[i], target)
        )
    result = total_w[band]
    for i in reversed(range(len(shifts))):
        band_copies[i].wait_recv()
        result = result + band_in[i].astype(jnp.float32)
    final[mine, line] = (result * scale).astype(jnp.bfloat16)

    def pass_on(m, l, send_sem, target):
        piece = final.at[m, l]
        send(piece, piece, send_sem, gather_recv.at[m, l], target)

    def arrive(m, l):
        piece = final.at[m, l]
        pltpu.make_async_copy(piece, piece, gather_recv.at[m, l]).wait()

    def spread(l, j):
        for i, step in reversed(list(enumerate(away_steps))):
            pass_on(mine, l, across_send.at[i, j], device(near(step, 1)))
        pass_on(mine, l, forward_send.at[0, j], partner)

    for i, m in enumerate(masks):
        pass_on(mine, line, along_send.at[i], along(m, pair))
    order = [0] + masks[::-1]
    spread(line, 0)
    for m in order[1:]:
        arrive(mine, flip(line, m))
        spread(flip(line, m), m)
    for m in order:
        for i, step in enumerate(away_steps):
            source = member(behind(step, 1))
            arrive(source, flip(line, m))
            pass_on(source, flip(line, m), forward_send.at[1 + i, m], partner)
    for step in [(0, 0)] + away_steps:
        source = member(behind(step, 1 if step == (0, 0) else 0))
        for m in order:
            arrive(source, flip(line, m))
    for copy in sends:
        copy.wait_send()
    for away, copy in row_copies:
        pl.when(away)(copy.wait_send)
    pl.when(not_first)(up_halo.wait_send)
    pl.when(not_last)(down_halo.wait_send)


def body(fields, embed_w, embed_b, merge_ids, ln_gain, w_up, w_down, d_out):
    bands = lax.axis_size("band")
    samples = lax.axis_size("sample")
    lon = merge_ids.shape[1]
    counts, starts = band_layout(bands, lon)
    shard_rows = starts[-1] // bands
    rotate = shard_rows - lon // 8
    granule = functools.reduce(math.gcd, counts + [rotate, shard_rows])
    features, model_width = embed_w.shape
    channels, lat_rows, cells = fields.shape[1:]
    pad_v = round_up(channels, 16)
    inner = 2 if bands <= 8 else 1
    lines, group = bands // inner, inner * samples
    part_rows = round_up(-(-(features + 1) // bands), 8)
    width = round_up(bands * part_rows, 128)
    vmem = pl.BlockSpec(memory_space=pltpu.VMEM)
    dma = pltpu.SemaphoreType.DMA

    scale = 1.0 / math.sqrt(samples * starts[-1])
    columns = model_width // samples
    hidden_width = w_up.shape[1]
    piece = (bands, part_rows, columns)
    away, side = group // 2 - 1, max(samples // 2 - 1, 1)
    bf16 = jnp.bfloat16
    hbm = pl.BlockSpec(memory_space=pl.ANY)
    f32 = jnp.float32
    mixed, final = pl.pallas_call(
        functools.partial(
            kernel, counts, rotate, shard_rows, features, granule, samples, inner, scale
        ),
        out_shape=(
            pltpu.VMEM((shard_rows, model_width), bf16),
            pltpu.VMEM((group, lines) + piece[1:], bf16),
        ),
        in_specs=[pl.BlockSpec(memory_space=pltpu.HBM)] * 8,
        out_specs=(vmem, vmem),
        scratch_shapes=[
            pltpu.VMEM(fields.shape[1:], bf16),
            pltpu.VMEM(merge_ids.shape, jnp.int32),
            pltpu.VMEM((1, model_width), f32),
            pltpu.VMEM((1, model_width), f32),
            pltpu.VMEM(embed_w.shape, bf16),
            pltpu.VMEM(w_up.shape, bf16),
            pltpu.VMEM(w_down.shape, bf16),
            pltpu.VMEM((shard_rows, model_width), bf16),
            pltpu.VMEM((4 * pad_v, cells), bf16),
            pltpu.VMEM((lon, width), bf16),
            pltpu.VMEM((samples, shard_rows, width), bf16),
            pltpu.VMEM((shard_rows, model_width), bf16),
            pltpu.VMEM((samples, shard_rows, columns), bf16),
            pltpu.VMEM((samples - 1, shard_rows, columns), bf16),
            pltpu.VMEM(piece, bf16),
            pltpu.VMEM((bands - 1,) + piece[1:], bf16),
            pltpu.VMEM(piece, f32),
            dma((8,)),
            dma((2,)),
            dma((2,)),
            dma((lon // granule,)),
            dma(()),
            dma((side + 1,)),
            dma((side,)),
            dma((samples,)),
            dma((samples - 1,)),
            dma((samples - 1,)),
            dma((bands - 1,)),
            dma((bands - 1,)),
            dma((lines - 1,)),
            dma((away, lines)),
            dma((away + 1, lines)),
            dma((group, lines)),
            pltpu.VMEM((shard_rows, hidden_width), bf16),
            pltpu.VMEM((shard_rows, hidden_width), bf16),
            pltpu.VMEM((shard_rows, model_width), jnp.float32),
        ],
        compiler_params=pltpu.CompilerParams(
            collective_id=0, has_side_effects=True, vmem_limit_bytes=32 << 20
        ),
    )(*[
        pltpu.with_memory_space_constraint(x, pltpu.HBM)
        for x in (
            fields[0], merge_ids, embed_b[None], ln_gain[None], embed_w, w_up, w_down, d_out[0]
        )
    ])
    mixed, grad, grad_b = pl.pallas_call(
        functools.partial(emit, inner),
        out_shape=(
            jax.ShapeDtypeStruct((shard_rows, model_width), bf16),
            jax.ShapeDtypeStruct((features, model_width), f32),
            jax.ShapeDtypeStruct((1, model_width), f32),
        ),
        in_specs=[vmem, vmem],
        out_specs=(hbm, hbm, hbm),
        scratch_shapes=[
            pltpu.VMEM((features, model_width), f32),
            pltpu.VMEM((1, model_width), f32),
            dma((2 + lines,)),
        ],
        compiler_params=pltpu.CompilerParams(vmem_limit_bytes=16 << 20),
    )(mixed, final)
    return mixed[None], grad, grad_b[0]


def solution(mesh):
    return jax.shard_map(
        body,
        mesh=mesh,
        in_specs=(
            P("sample", None, "band", None),
            P(),
            P(),
            P("band", None),
            P(),
            P(),
            P(),
            P("sample", "band", None),
        ),
        out_specs=(P("sample", "band", None), P(), P()),
        check_vma=False,
    )
```

```python
import functools
import math

import jax
import jax.numpy as jnp
from jax import lax
from jax.experimental import pallas as pl
from jax.experimental.pallas import tpu as pltpu
from jax.sharding import PartitionSpec as P

MESH = pl.DeviceIdType.MESH


def round_up(value, step):
    return -(-value // step) * step


def band_layout(band_total, lon_patches):
    counts = []
    for b in range(band_total):
        distance = min(b, band_total - 1 - b)
        factor = 4 if distance < band_total // 8 else 2 if distance < band_total // 4 else 1
        counts.append(lon_patches // factor)
    starts = [0]
    for c in counts:
        starts.append(starts[-1] + c)
    return (counts, starts)


def flip(value, mask):
    for bit in range(mask.bit_length()):
        if mask >> bit & 1:
            value = value + (1 - 2 * lax.rem(lax.div(value, 1 << bit), 2)) * (1 << bit)
    return value


def emit(inner, mixed_ref, final_ref, mixed_out, w_out, b_out, staged, b_staged, sems):
    members, lines, part_rows, columns = final_ref.shape
    blocks = members // inner
    features = w_out.shape[0]
    copies = [pltpu.make_async_copy(mixed_ref, mixed_out, sems.at[0])]
    copies[0].start()
    for line in range(lines):
        start = line * inner * part_rows
        for pair in range(inner):
            low = start + pair * part_rows
            rows = min(part_rows, features - low)
            for m in range(blocks):
                values = final_ref[pair * blocks + m, line].astype(jnp.float32)
                if rows > 0:
                    staged[low : low + rows, m * columns : (m + 1) * columns] = values[:rows]
                if low <= features < low + part_rows:
                    b_staged[:, m * columns : (m + 1) * columns] = values[
                        features - low : features - low + 1
                    ]
        rows = min(inner * part_rows, features - start)
        if rows > 0:
            span = pl.ds(start, rows)
            copy = pltpu.make_async_copy(staged.at[span], w_out.at[span], sems.at[2 + line])
            copy.start()
            copies.append(copy)
    copies.append(pltpu.make_async_copy(b_staged, b_out, sems.at[1]))
    copies[-1].start()
    for copy in copies:
        copy.wait()


def kernel(
    counts, rotate, shard_rows, features, granule, samples, inner, scale,
    own_hbm, ids_hbm, bias_hbm, gain_hbm, embed_hbm, up_hbm, down_hbm, cot_hbm,
    mixed_ref, final,
    own_ref, ids_ref, bias_ref, gain_ref,
    embed, up, down, cot, grid, packed, rows_all, normed, grads, grads_in,
    band_out, band_in, total_w,
    load, halo_send, halo_recv, row_send, row_recv,
    rows_send, rows_forward, rows_done, grads_send, grads_recv,
    band_send, band_recv, along_send, across_send, forward_send, forward_recv, gather_recv,
    d_hid, hid, held_tokens, known,
):
    total = len(counts)
    lines, chips = total // inner, samples // 2
    band, sample = lax.axis_index("band"), lax.axis_index("sample")
    line, pair = lax.div(band, inner), lax.rem(band, inner)
    chip, core = lax.div(sample, 2), lax.rem(sample, 2)
    half = lax.div(line, lines // 2)
    other = 1 - core
    partner = (band, 2 * chip + other)

    def near(step, turn):
        p, c = step
        return (lax.rem(pair + p, inner), lax.rem(chip + c, chips), core if turn == 0 else other)

    def behind(step, turn):
        p, c = step
        return (
            lax.rem(pair + inner - p, inner),
            lax.rem(chip + chips - c, chips),
            core if turn == 0 else other,
        )

    def device(spot):
        p, c, k = spot
        return (line * inner + p, 2 * c + k)

    def block(spot):
        p, c, k = spot
        return 2 * c + lax.rem(k + half, 2)

    def member(spot):
        return spot[0] * samples + block(spot)

    steps = [(p, c) for p in range(inner) for c in range(chips)]
    away_steps = sorted(steps[1:], key=lambda step: (step[0] > 0) + (step[1] > 0))
    here_spot = (pair, chip, core)
    my_block, mine = block(here_spot), member(here_spot)
    side_steps = [step for step in away_steps if step[0] == 0]
    peer_keys = [((0, 0), 1)] + [(step, turn) for step in side_steps for turn in (1, 0)]
    masks = sorted(range(1, lines), reverse=True)

    def along(mask, p):
        return (flip(line, mask) * inner + p, 2 * chip + (other if 2 * mask >= lines else core))

    shifts = [(mask, p) for mask in masks for p in reversed(range(inner))]
    shifts += [(0, p) for p in range(1, inner)]

    def turned(p):
        return lax.rem(pair + p, inner)


    def beside(reach):
        return [(lax.rem(band + o, total), sample) for o in {reach, total - reach}]

    def say(i, devices):
        for target in devices:
            pl.semaphore_signal(known.at[i], inc=1, device_id=target, device_id_type=MESH)

    plane = [partner] + [device(near(step, turn)) for step in side_steps for turn in (0, 1)]
    reaches = [1 << i for i in range((total - 1).bit_length() - 1)]
    greeted = beside(1) + plane
    barrier = pltpu.get_barrier_semaphore()
    for peer in greeted:
        pl.semaphore_signal(barrier, inc=1, device_id=peer, device_id_type=MESH)

    loads = [
        pltpu.make_async_copy(src, dst, load.at[i])
        for i, (src, dst) in enumerate(
            (
                (embed_hbm, embed), (up_hbm, up), (down_hbm, down), (cot_hbm, cot),
                (own_hbm, own_ref), (ids_hbm, ids_ref), (bias_hbm, bias_ref), (gain_hbm, gain_ref),
            )
        )
    ]
    for i in (4, 5, 3, 2, 0, 6, 7, 1):
        loads[i].start()
    def remote(src, dst, send, recv, device):
        return pltpu.make_async_remote_copy(
            src_ref=src, dst_ref=dst, send_sem=send, recv_sem=recv,
            device_id=device, device_id_type=MESH,
        )

    pad_v = grid.shape[0] // 4
    landed = rows_all.at[sample]
    up_halo = remote(
        grid.at[pl.ds(pad_v, pad_v)], grid.at[pl.ds(3 * pad_v, pad_v)],
        halo_send.at[0], halo_recv.at[0], (lax.rem(band + total - 1, total), sample),
    )
    down_halo = remote(
        grid.at[pl.ds(2 * pad_v, pad_v)], grid.at[pl.ds(0, pad_v)],
        halo_send.at[1], halo_recv.at[1], (lax.rem(band + 1, total), sample),
    )
    is_first, is_last = band == 0, band == total - 1
    not_first, not_last = band > 0, band < total - 1
    channels = own_ref.shape[0]
    loads[4].wait()
    grid[pl.ds(pad_v, 2 * pad_v), :] = jnp.zeros((2 * pad_v, grid.shape[1]), grid.dtype)
    for r in range(2):
        grid[pl.ds((1 + r) * pad_v, channels), :] = own_ref[:, r, :]
    lon, cells, width = packed.shape[0], grid.shape[1], packed.shape[1]
    slot = lax.broadcasted_iota(jnp.int32, (lon, lon), 0)
    loads[5].wait()
    onehot = (ids_ref[...] == slot).astype(jnp.float32)
    members = jnp.sum(onehot, axis=1, keepdims=True)
    safe = jnp.where(members > 0, members, 1.0)
    onehot = onehot.astype(jnp.bfloat16)
    patch = lax.broadcasted_iota(jnp.int32, (lon, cells), 0)
    cell = lax.broadcasted_iota(jnp.int32, (lon, cells), 1)
    picks = [
        jnp.dot(
            onehot, (cell == 2 * patch + q).astype(jnp.float32).astype(jnp.bfloat16),
            preferred_element_type=jnp.float32,
        ).astype(jnp.bfloat16)
        for q in range(2)
    ]
    rows = lax.broadcasted_iota(jnp.int32, (4 * pad_v, width), 0)
    column = lax.broadcasted_iota(jnp.int32, (4 * pad_v, width), 1)
    r = (
        (rows >= pad_v).astype(jnp.int32)
        + (rows >= 2 * pad_v).astype(jnp.int32)
        + (rows >= 3 * pad_v).astype(jnp.int32)
    )
    place = 8 * (rows - pad_v * r) + 2 * r
    moves = [(column == place + q).astype(jnp.float32).astype(jnp.bfloat16) for q in range(2)]
    pl.semaphore_wait(barrier, len(greeted))
    say(0, beside(1))
    pl.when(not_first)(up_halo.start)
    pl.when(not_last)(down_halo.start)

    @pl.when(is_first)
    def _():
        grid[pl.ds(0, pad_v), :] = jnp.zeros((pad_v, grid.shape[1]), grid.dtype)

    @pl.when(is_last)
    def _():
        grid[pl.ds(3 * pad_v, pad_v), :] = jnp.zeros((pad_v, grid.shape[1]), grid.dtype)

    pl.when(not_last)(up_halo.wait_recv)
    pl.when(not_first)(down_halo.wait_recv)
    ordered = None
    for q in range(2):
        summed = lax.dot_general(
            picks[q], grid[...], (((1,), (1,)), ((), ())), preferred_element_type=jnp.float32
        )
        mean = (summed / safe).astype(jnp.bfloat16)
        part = jnp.dot(mean, moves[q], preferred_element_type=jnp.float32)
        ordered = part if ordered is None else ordered + part
    ones = lax.broadcasted_iota(jnp.int32, (lon, width), 1) == features
    packed[...] = jnp.where(ones, 1.0, ordered).astype(packed.dtype)

    pl.semaphore_wait(known.at[0], len(beside(1)))
    say(1, beside(2))
    my_count = sum(jnp.where(band == b, c, 0) for b, c in enumerate(counts))
    my_start = rotate + sum(jnp.where(band > b, c, 0) for b, c in enumerate(counts))
    row_copies = []
    for i in range(lon // granule):
        unwrapped = my_start + granule * i
        target = lax.rem(lax.div(unwrapped, shard_rows), total)
        offset = pl.multiple_of(lax.rem(unwrapped, shard_rows), granule)
        valid = granule * i < my_count
        here = target == band
        src, dst = packed.at[pl.ds(granule * i, granule)], landed.at[pl.ds(offset, granule)]
        copy = remote(src, dst, row_send.at[i], row_recv, (target, sample))
        keep = pltpu.make_async_copy(src, dst, row_recv)
        away = jnp.logical_and(valid, jnp.logical_not(here))
        pl.when(away)(copy.start)
        pl.when(jnp.logical_and(valid, here))(keep.start)
        row_copies.append((away, copy))
    for i in (2, 3):
        loads[i].wait()
    hidden_width = up.shape[1]
    tile = 512
    across = (((1,), (1,)), ((), ()))
    for t in range(hidden_width // tile):
        span = slice(t * tile, (t + 1) * tile)
        d_hid[:, span] = lax.dot_general(
            cot[...], down[span, :], across, preferred_element_type=jnp.float32
        ).astype(jnp.bfloat16)
    for i, reach in enumerate(reaches[1:]):
        pl.semaphore_wait(known.at[i + 1], len(beside(reach)))
        say(i + 2, beside(2 * reach) if 2 * reach in reaches else plane)
    pltpu.make_async_copy(landed, landed, row_recv).wait()

    def send(src, dst, send_sem, recv_sem, target):
        copy = remote(src, dst, send_sem, recv_sem, target)
        copy.start()
        return copy

    def settle(ref, semaphore):
        pltpu.make_async_copy(ref, ref, semaphore).wait()

    def send_rows(m, send_sem, target):
        send(rows_all.at[m], rows_all.at[m], send_sem, rows_done.at[m], target)

    def rows_arrive(m):
        pltpu.make_async_copy(rows_all.at[m], rows_all.at[m], rows_done.at[m]).wait()

    for step in side_steps:
        send_rows(sample, rows_send, device(near(step, 1)))
    send_rows(sample, rows_send, partner)

    for i in (0, 6, 7):
        loads[i].wait()
    tokens = (
        jnp.dot(landed[:, :features], embed[...], preferred_element_type=jnp.float32)
        + bias_ref[...]
    ).astype(jnp.bfloat16).astype(jnp.float32)
    model_width = tokens.shape[1]
    centred = tokens - jnp.mean(tokens, axis=-1, keepdims=True)
    inverse = lax.rsqrt(jnp.mean(centred * centred, axis=-1, keepdims=True) + 1e-05)
    normed[...] = (centred * inverse * gain_ref[...]).astype(jnp.bfloat16)
    held_tokens[...] = tokens
    d_normed = jnp.zeros_like(tokens)
    loads[1].wait()
    slope = math.sqrt(2.0 / math.pi)
    for t in range(hidden_width // tile):
        span = slice(t * tile, (t + 1) * tile)
        pre = jnp.dot(normed[...], up[:, span], preferred_element_type=jnp.float32)
        d_hidden = d_hid[:, span].astype(jnp.float32)
        square = pre * pre
        bent = jnp.tanh(slope * (pre + 0.044715 * (square * pre)))
        cdf = 0.5 * (1.0 + bent)
        hid[:, span] = (pre * cdf).astype(jnp.bfloat16)
        steep = cdf + (0.5 * slope) * pre * (1.0 - bent * bent) * (
            1.0 + (3.0 * 0.044715) * square
        )
        d_pre = (d_hidden * steep).astype(jnp.bfloat16)
        d_normed = d_normed + lax.dot_general(
            d_pre, up[:, span], across, preferred_element_type=jnp.float32
        )
    d_scaled = d_normed.astype(jnp.bfloat16).astype(jnp.float32) * gain_ref[...]
    d_var = jnp.sum(d_scaled * centred, axis=-1, keepdims=True) * (
        -0.5 * inverse * inverse * inverse
    )
    d_centred = d_scaled * inverse + centred * (d_var * (2.0 / model_width))
    d_tokens = d_centred - jnp.mean(d_centred, axis=-1, keepdims=True)
    grad = (cot[...].astype(jnp.float32) + d_tokens).astype(jnp.bfloat16)
    columns = grads.shape[2]
    for m in range(samples):
        grads[m] = grad[:, m * columns : (m + 1) * columns]

    grad_copies = {}
    for i, key in reversed(list(enumerate(peer_keys))):
        spot = near(*key)
        grad_copies[key] = send(
            grads.at[block(spot)], grads_in.at[i], grads_send, grads_recv.at[i],
            device(spot),
        )

    mixed = held_tokens[...]
    for t in range(hidden_width // tile):
        span = slice(t * tile, (t + 1) * tile)
        mixed = mixed + jnp.dot(hid[:, span], down[span, :], preferred_element_type=jnp.float32)
    mixed_ref[...] = mixed.astype(jnp.bfloat16)
    part_rows = total_w.shape[1]
    span_rows = total * part_rows

    def product(s, values):
        full = lax.dot_general(
            rows_all[s], values, (((0,), (0,)), ((), ())), preferred_element_type=jnp.float32
        )
        return full[:span_rows].reshape(total, part_rows, columns)

    def origin(key):
        return device(behind(*key))[1]

    def add_product(key):
        grad_copies[key].wait_recv()
        total_w[...] += product(origin(key), grads_in[peer_keys.index(key)])

    total_w[...] = product(sample, grads[my_block])
    rows_arrive(origin(((0, 0), 1)))
    add_product(((0, 0), 1))
    for i, step in enumerate(side_steps):
        source = origin((step, 1))
        rows_arrive(source)
        send_rows(source, rows_forward, partner)
        add_product((step, 1))
    for step in side_steps:
        rows_arrive(origin((step, 0)))
        add_product((step, 0))

    pl.semaphore_wait(known.at[len(reaches)], len(plane))
    band_copies = []
    for i, (m, p) in enumerate(shifts):
        target = along(m, turned(p))
        band_out[target[0]] = total_w[target[0]].astype(jnp.bfloat16)
        band_copies.append(
            send(band_out.at[target[0]], band_in.at[i], band_send, band_recv.at[i], target)
        )
    result = total_w[band]
    for i in reversed(range(len(shifts))):
        band_copies[i].wait_recv()
        result = result + band_in[i].astype(jnp.float32)
    final[mine, line] = (result * scale).astype(jnp.bfloat16)

    def pass_on(m, l, send_sem, recv_sem, target):
        piece = final.at[m, l]
        send(piece, piece, send_sem, recv_sem, target)

    def arrive(m, l):
        settle(final.at[m, l], gather_recv.at[m, l])

    def spread(l):
        for step in reversed(away_steps):
            pass_on(mine, l, across_send, gather_recv.at[mine, l], device(near(step, 1)))
        pass_on(mine, l, forward_send, forward_recv, partner)

    for m in masks:
        pass_on(mine, line, along_send, gather_recv.at[mine, line], along(m, pair))
    order = [0] + masks[::-1]
    spread(line)
    settle(band_out.at[: total - 1], band_send)
    settle(grads.at[: samples - 1], grads_send)
    settle(rows_all.at[: len(side_steps) + 1], rows_send)
    if side_steps:
        settle(rows_all.at[: len(side_steps)], rows_forward)
    for away, copy in row_copies:
        pl.when(away)(copy.wait_send)
    pl.when(not_first)(up_halo.wait_send)
    pl.when(not_last)(down_halo.wait_send)
    for m in order[1:]:
        arrive(mine, flip(line, m))
        spread(flip(line, m))
    settle(final.at[0, : lines - 1], along_send)
    for m in order:
        for step in away_steps:
            source = member(behind(step, 1))
            arrive(source, flip(line, m))
            pass_on(source, flip(line, m), forward_send, forward_recv, partner)
    settle(final.at[: len(away_steps)], across_send)
    settle(final.at[: len(away_steps) + 1], forward_send)
    settle(final.at[: len(away_steps) + 1], forward_recv)


def body(fields, embed_w, embed_b, merge_ids, ln_gain, w_up, w_down, d_out):
    bands = lax.axis_size("band")
    samples = lax.axis_size("sample")
    lon = merge_ids.shape[1]
    counts, starts = band_layout(bands, lon)
    shard_rows = starts[-1] // bands
    rotate = shard_rows - lon // 8
    granule = functools.reduce(math.gcd, counts + [rotate, shard_rows])
    features, model_width = embed_w.shape
    channels, lat_rows, cells = fields.shape[1:]
    pad_v = round_up(channels, 16)
    inner = 2 if bands <= 8 else 1
    lines, group = bands // inner, inner * samples
    part_rows = round_up(-(-(features + 1) // bands), 8)
    width = round_up(bands * part_rows, 128)
    vmem = pl.BlockSpec(memory_space=pltpu.VMEM)
    dma = pltpu.SemaphoreType.DMA

    scale = 1.0 / math.sqrt(samples * starts[-1])
    columns = model_width // samples
    hidden_width = w_up.shape[1]
    piece = (bands, part_rows, columns)
    bf16 = jnp.bfloat16
    hbm = pl.BlockSpec(memory_space=pl.ANY)
    f32 = jnp.float32
    mixed, final = pl.pallas_call(
        functools.partial(
            kernel, counts, rotate, shard_rows, features, granule, samples, inner, scale
        ),
        out_shape=(
            pltpu.VMEM((shard_rows, model_width), bf16),
            pltpu.VMEM((group, lines) + piece[1:], bf16),
        ),
        in_specs=[pl.BlockSpec(memory_space=pltpu.HBM)] * 8,
        out_specs=(vmem, vmem),
        scratch_shapes=[
            pltpu.VMEM(fields.shape[1:], bf16),
            pltpu.VMEM(merge_ids.shape, jnp.int32),
            pltpu.VMEM((1, model_width), f32),
            pltpu.VMEM((1, model_width), f32),
            pltpu.VMEM(embed_w.shape, bf16),
            pltpu.VMEM(w_up.shape, bf16),
            pltpu.VMEM(w_down.shape, bf16),
            pltpu.VMEM((shard_rows, model_width), bf16),
            pltpu.VMEM((4 * pad_v, cells), bf16),
            pltpu.VMEM((lon, width), bf16),
            pltpu.VMEM((samples, shard_rows, width), bf16),
            pltpu.VMEM((shard_rows, model_width), bf16),
            pltpu.VMEM((samples, shard_rows, columns), bf16),
            pltpu.VMEM((samples - 1, shard_rows, columns), bf16),
            pltpu.VMEM(piece, bf16),
            pltpu.VMEM((bands - 1,) + piece[1:], bf16),
            pltpu.VMEM(piece, f32),
            dma((8,)),
            dma((2,)),
            dma((2,)),
            dma((lon // granule,)),
            dma(()),
            dma(()),
            dma(()),
            dma((samples,)),
            dma(()),
            dma((samples - 1,)),
            dma(()),
            dma((bands - 1,)),
            dma(()),
            dma(()),
            dma(()),
            dma(()),
            dma((group, lines)),
            pltpu.VMEM((shard_rows, hidden_width), bf16),
            pltpu.VMEM((shard_rows, hidden_width), bf16),
            pltpu.VMEM((shard_rows, model_width), jnp.float32),
            pltpu.SemaphoreType.REGULAR(((bands - 1).bit_length(),)),
        ],
        compiler_params=pltpu.CompilerParams(
            collective_id=0, has_side_effects=True, vmem_limit_bytes=32 << 20
        ),
    )(*[
        pltpu.with_memory_space_constraint(x, pltpu.HBM)
        for x in (
            fields[0], merge_ids, embed_b[None], ln_gain[None], embed_w, w_up, w_down, d_out[0]
        )
    ])
    mixed, grad, grad_b = pl.pallas_call(
        functools.partial(emit, inner),
        out_shape=(
            jax.ShapeDtypeStruct((shard_rows, model_width), bf16),
            jax.ShapeDtypeStruct((features, model_width), f32),
            jax.ShapeDtypeStruct((1, model_width), f32),
        ),
        in_specs=[vmem, vmem],
        out_specs=(hbm, hbm, hbm),
        scratch_shapes=[
            pltpu.VMEM((features, model_width), f32),
            pltpu.VMEM((1, model_width), f32),
            dma((2 + lines,)),
        ],
        compiler_params=pltpu.CompilerParams(vmem_limit_bytes=16 << 20),
    )(mixed, final)
    return mixed[None], grad, grad_b[0]


def solution(mesh):
    return jax.shard_map(
        body,
        mesh=mesh,
        in_specs=(
            P("sample", None, "band", None),
            P(),
            P(),
            P("band", None),
            P(),
            P(),
            P(),
            P("sample", "band", None),
        ),
        out_specs=(P("sample", "band", None), P(), P()),
        check_vma=False,
    )
```

```python
import functools
import math

import jax
import jax.numpy as jnp
from jax import lax
from jax.experimental import pallas as pl
from jax.experimental.pallas import tpu as pltpu
from jax.sharding import PartitionSpec as P

MESH = pl.DeviceIdType.MESH


def round_up(value, step):
    return -(-value // step) * step


def band_layout(band_total, lon_patches):
    counts = []
    for b in range(band_total):
        distance = min(b, band_total - 1 - b)
        factor = 4 if distance < band_total // 8 else 2 if distance < band_total // 4 else 1
        counts.append(lon_patches // factor)
    starts = [0]
    for c in counts:
        starts.append(starts[-1] + c)
    return (counts, starts)


def flip(value, mask):
    for bit in range(mask.bit_length()):
        if mask >> bit & 1:
            value = value + (1 - 2 * lax.rem(lax.div(value, 1 << bit), 2)) * (1 << bit)
    return value


def emit(inner, mixed_ref, final_ref, mixed_out, w_out, b_out, staged, b_staged, sems):
    members, lines, part_rows, columns = final_ref.shape
    blocks = members // inner
    features = w_out.shape[0]
    copies = [pltpu.make_async_copy(mixed_ref, mixed_out, sems.at[0])]
    copies[0].start()
    for line in range(lines):
        start = line * inner * part_rows
        for pair in range(inner):
            low = start + pair * part_rows
            rows = min(part_rows, features - low)
            for m in range(blocks):
                values = final_ref[pair * blocks + m, line].astype(jnp.float32)
                if rows > 0:
                    staged[low : low + rows, m * columns : (m + 1) * columns] = values[:rows]
                if low <= features < low + part_rows:
                    b_staged[:, m * columns : (m + 1) * columns] = values[
                        features - low : features - low + 1
                    ]
        rows = min(inner * part_rows, features - start)
        if rows > 0:
            span = pl.ds(start, rows)
            copy = pltpu.make_async_copy(staged.at[span], w_out.at[span], sems.at[2 + line])
            copy.start()
            copies.append(copy)
    copies.append(pltpu.make_async_copy(b_staged, b_out, sems.at[1]))
    copies[-1].start()
    for copy in copies:
        copy.wait()


def kernel(
    counts, rotate, shard_rows, features, granule, samples, inner, scale,
    own_hbm, ids_hbm, bias_hbm, gain_hbm, embed_hbm, up_hbm, down_hbm, cot_hbm,
    mixed_ref, final,
    own_ref, ids_ref, bias_ref, gain_ref,
    embed, up, down, cot, grid, packed, rows_all, normed, grads, grads_in,
    band_out, band_in, total_w,
    load, halo_send, halo_recv, row_send, row_recv,
    rows_send, rows_forward, rows_done, grads_send, grads_recv,
    band_send, band_recv, along_send, across_send, forward_send, forward_recv, gather_recv,
    d_hid, hid, held_tokens, known,
):
    total = len(counts)
    lines, chips = total // inner, samples // 2
    band, sample = lax.axis_index("band"), lax.axis_index("sample")
    line, pair = lax.div(band, inner), lax.rem(band, inner)
    chip, core = lax.div(sample, 2), lax.rem(sample, 2)
    half = lax.div(line, lines // 2)
    other = 1 - core
    partner = (band, 2 * chip + other)

    def near(step, turn):
        p, c = step
        return (lax.rem(pair + p, inner), lax.rem(chip + c, chips), core if turn == 0 else other)

    def behind(step, turn):
        p, c = step
        return (
            lax.rem(pair + inner - p, inner),
            lax.rem(chip + chips - c, chips),
            core if turn == 0 else other,
        )

    def device(spot):
        p, c, k = spot
        return (line * inner + p, 2 * c + k)

    def block(spot):
        p, c, k = spot
        return 2 * c + lax.rem(k + half, 2)

    def member(spot):
        return spot[0] * samples + block(spot)

    steps = [(p, c) for p in range(inner) for c in range(chips)]
    away_steps = sorted(steps[1:], key=lambda step: (step[0] > 0) + (step[1] > 0))
    here_spot = (pair, chip, core)
    my_block, mine = block(here_spot), member(here_spot)
    side_steps = [step for step in away_steps if step[0] == 0]
    peer_keys = [((0, 0), 1)] + [(step, turn) for step in side_steps for turn in (1, 0)]
    masks = sorted(range(1, lines), reverse=True)

    def along(mask, p):
        return (flip(line, mask) * inner + p, 2 * chip + (other if 2 * mask >= lines else core))

    shifts = [(mask, p) for mask in masks for p in reversed(range(inner))]
    shifts += [(0, p) for p in range(1, inner)]

    def turned(p):
        return lax.rem(pair + p, inner)


    def beside(reach):
        return [(lax.rem(band + o, total), sample) for o in {reach, total - reach}]

    def say(i, devices):
        for target in devices:
            pl.semaphore_signal(known.at[i], inc=1, device_id=target, device_id_type=MESH)

    plane = [partner] + [device(near(step, turn)) for step in side_steps for turn in (0, 1)]
    reaches = [1 << i for i in range((total - 1).bit_length() - 1)]
    greeted = beside(1) + plane
    barrier = pltpu.get_barrier_semaphore()
    for peer in greeted:
        pl.semaphore_signal(barrier, inc=1, device_id=peer, device_id_type=MESH)

    loads = [
        pltpu.make_async_copy(src, dst, load.at[i])
        for i, (src, dst) in enumerate(
            (
                (embed_hbm, embed), (up_hbm, up), (down_hbm, down), (cot_hbm, cot),
                (own_hbm, own_ref), (ids_hbm, ids_ref), (bias_hbm, bias_ref), (gain_hbm, gain_ref),
            )
        )
    ]
    for i in (4, 5, 3, 2, 0, 6, 7, 1):
        loads[i].start()
    def remote(src, dst, send, recv, device):
        return pltpu.make_async_remote_copy(
            src_ref=src, dst_ref=dst, send_sem=send, recv_sem=recv,
            device_id=device, device_id_type=MESH,
        )

    pad_v = grid.shape[0] // 4
    landed = rows_all.at[sample]
    up_halo = remote(
        grid.at[pl.ds(pad_v, pad_v)], grid.at[pl.ds(3 * pad_v, pad_v)],
        halo_send.at[0], halo_recv.at[0], (lax.rem(band + total - 1, total), sample),
    )
    down_halo = remote(
        grid.at[pl.ds(2 * pad_v, pad_v)], grid.at[pl.ds(0, pad_v)],
        halo_send.at[1], halo_recv.at[1], (lax.rem(band + 1, total), sample),
    )
    is_first, is_last = band == 0, band == total - 1
    not_first, not_last = band > 0, band < total - 1
    channels = own_ref.shape[0]
    loads[4].wait()
    grid[pl.ds(pad_v, 2 * pad_v), :] = jnp.zeros((2 * pad_v, grid.shape[1]), grid.dtype)
    for r in range(2):
        grid[pl.ds((1 + r) * pad_v, channels), :] = own_ref[:, r, :]
    lon, cells, width = packed.shape[0], grid.shape[1], packed.shape[1]
    slot = lax.broadcasted_iota(jnp.int32, (lon, lon), 0)
    loads[5].wait()
    onehot = (ids_ref[...] == slot).astype(jnp.float32)
    members = jnp.sum(onehot, axis=1, keepdims=True)
    safe = jnp.where(members > 0, members, 1.0)
    onehot = onehot.astype(jnp.bfloat16)
    patch = lax.broadcasted_iota(jnp.int32, (lon, cells), 0)
    cell = lax.broadcasted_iota(jnp.int32, (lon, cells), 1)
    picks = [
        jnp.dot(
            onehot, (cell == 2 * patch + q).astype(jnp.float32).astype(jnp.bfloat16),
            preferred_element_type=jnp.float32,
        ).astype(jnp.bfloat16)
        for q in range(2)
    ]
    rows = lax.broadcasted_iota(jnp.int32, (4 * pad_v, width), 0)
    column = lax.broadcasted_iota(jnp.int32, (4 * pad_v, width), 1)
    r = (
        (rows >= pad_v).astype(jnp.int32)
        + (rows >= 2 * pad_v).astype(jnp.int32)
        + (rows >= 3 * pad_v).astype(jnp.int32)
    )
    place = 8 * (rows - pad_v * r) + 2 * r
    moves = [(column == place + q).astype(jnp.float32).astype(jnp.bfloat16) for q in range(2)]
    pl.semaphore_wait(barrier, len(greeted))
    say(0, beside(1))
    pl.when(not_first)(up_halo.start)
    pl.when(not_last)(down_halo.start)

    @pl.when(is_first)
    def _():
        grid[pl.ds(0, pad_v), :] = jnp.zeros((pad_v, grid.shape[1]), grid.dtype)

    @pl.when(is_last)
    def _():
        grid[pl.ds(3 * pad_v, pad_v), :] = jnp.zeros((pad_v, grid.shape[1]), grid.dtype)

    pl.when(not_last)(up_halo.wait_recv)
    pl.when(not_first)(down_halo.wait_recv)
    ordered = None
    for q in range(2):
        summed = lax.dot_general(
            picks[q], grid[...], (((1,), (1,)), ((), ())), preferred_element_type=jnp.float32
        )
        mean = (summed / safe).astype(jnp.bfloat16)
        part = jnp.dot(mean, moves[q], preferred_element_type=jnp.float32)
        ordered = part if ordered is None else ordered + part
    ones = lax.broadcasted_iota(jnp.int32, (lon, width), 1) == features
    packed[...] = jnp.where(ones, 1.0, ordered).astype(packed.dtype)

    pl.semaphore_wait(known.at[0], len(beside(1)))
    say(1, beside(2))
    my_count = sum(jnp.where(band == b, c, 0) for b, c in enumerate(counts))
    my_start = rotate + sum(jnp.where(band > b, c, 0) for b, c in enumerate(counts))
    row_copies = []
    for i in range(lon // granule):
        unwrapped = my_start + granule * i
        target = lax.rem(lax.div(unwrapped, shard_rows), total)
        offset = pl.multiple_of(lax.rem(unwrapped, shard_rows), granule)
        valid = granule * i < my_count
        here = target == band
        src, dst = packed.at[pl.ds(granule * i, granule)], landed.at[pl.ds(offset, granule)]
        copy = remote(src, dst, row_send.at[i], row_recv, (target, sample))
        keep = pltpu.make_async_copy(src, dst, row_recv)
        away = jnp.logical_and(valid, jnp.logical_not(here))
        pl.when(away)(copy.start)
        pl.when(jnp.logical_and(valid, here))(keep.start)
        row_copies.append((away, copy))
    for i in (2, 3):
        loads[i].wait()
    hidden_width = up.shape[1]
    tile = 512
    across = (((1,), (1,)), ((), ()))
    for t in range(hidden_width // tile):
        span = slice(t * tile, (t + 1) * tile)
        d_hid[:, span] = lax.dot_general(
            cot[...], down[span, :], across, preferred_element_type=jnp.float32
        ).astype(jnp.bfloat16)
    for i, reach in enumerate(reaches[1:]):
        pl.semaphore_wait(known.at[i + 1], len(beside(reach)))
        say(i + 2, beside(2 * reach) if 2 * reach in reaches else plane)
    pltpu.make_async_copy(landed, landed, row_recv).wait()

    def send(src, dst, send_sem, recv_sem, target):
        copy = remote(src, dst, send_sem, recv_sem, target)
        copy.start()
        return copy

    def settle(ref, semaphore):
        pltpu.make_async_copy(ref, ref, semaphore).wait()

    def send_rows(m, send_sem, target):
        send(rows_all.at[m], rows_all.at[m], send_sem, rows_done.at[m], target)

    def rows_arrive(m):
        pltpu.make_async_copy(rows_all.at[m], rows_all.at[m], rows_done.at[m]).wait()

    for step in side_steps:
        send_rows(sample, rows_send, device(near(step, 1)))
    send_rows(sample, rows_send, partner)

    for i in (0, 6, 7):
        loads[i].wait()
    tokens = (
        jnp.dot(landed[:, :features], embed[...], preferred_element_type=jnp.float32)
        + bias_ref[...]
    ).astype(jnp.bfloat16).astype(jnp.float32)
    model_width = tokens.shape[1]
    centred = tokens - jnp.mean(tokens, axis=-1, keepdims=True)
    inverse = lax.rsqrt(jnp.mean(centred * centred, axis=-1, keepdims=True) + 1e-05)
    normed[...] = (centred * inverse * gain_ref[...]).astype(jnp.bfloat16)
    held_tokens[...] = tokens
    d_normed = jnp.zeros_like(tokens)
    loads[1].wait()
    slope = math.sqrt(2.0 / math.pi)
    for t in range(hidden_width // tile):
        span = slice(t * tile, (t + 1) * tile)
        pre = jnp.dot(normed[...], up[:, span], preferred_element_type=jnp.float32)
        d_hidden = d_hid[:, span].astype(jnp.float32)
        bend = (slope * 0.044715) * (pre * pre)
        inner_arg = pre * (bend + slope)
        bent = jnp.tanh(inner_arg)
        cdf = 0.5 * bent + 0.5
        hid[:, span] = (pre * cdf).astype(jnp.bfloat16)
        steep = cdf * ((1.0 - bent) * (inner_arg + (pre + pre) * bend) + 1.0)
        d_pre = (d_hidden * steep).astype(jnp.bfloat16)
        d_normed = d_normed + lax.dot_general(
            d_pre, up[:, span], across, preferred_element_type=jnp.float32
        )
    d_scaled = d_normed.astype(jnp.bfloat16).astype(jnp.float32) * gain_ref[...]
    d_var = jnp.sum(d_scaled * centred, axis=-1, keepdims=True) * (
        -0.5 * inverse * inverse * inverse
    )
    d_centred = d_scaled * inverse + centred * (d_var * (2.0 / model_width))
    d_tokens = d_centred - jnp.mean(d_centred, axis=-1, keepdims=True)
    grad = (cot[...].astype(jnp.float32) + d_tokens).astype(jnp.bfloat16)
    columns = grads.shape[2]
    for m in range(samples):
        grads[m] = grad[:, m * columns : (m + 1) * columns]

    grad_copies = {}
    for i, key in reversed(list(enumerate(peer_keys))):
        spot = near(*key)
        grad_copies[key] = send(
            grads.at[block(spot)], grads_in.at[i], grads_send, grads_recv.at[i],
            device(spot),
        )

    mixed = held_tokens[...]
    for t in range(hidden_width // tile):
        span = slice(t * tile, (t + 1) * tile)
        mixed = mixed + jnp.dot(hid[:, span], down[span, :], preferred_element_type=jnp.float32)
    mixed_ref[...] = mixed.astype(jnp.bfloat16)
    part_rows = total_w.shape[1]
    span_rows = total * part_rows

    def product(s, values):
        full = lax.dot_general(
            rows_all[s], values, (((0,), (0,)), ((), ())), preferred_element_type=jnp.float32
        )
        return full[:span_rows].reshape(total, part_rows, columns)

    def origin(key):
        return device(behind(*key))[1]

    def add_product(key):
        grad_copies[key].wait_recv()
        total_w[...] += product(origin(key), grads_in[peer_keys.index(key)])

    total_w[...] = product(sample, grads[my_block])
    rows_arrive(origin(((0, 0), 1)))
    add_product(((0, 0), 1))
    for i, step in enumerate(side_steps):
        source = origin((step, 1))
        rows_arrive(source)
        send_rows(source, rows_forward, partner)
        add_product((step, 1))
    for step in side_steps:
        rows_arrive(origin((step, 0)))
        add_product((step, 0))

    pl.semaphore_wait(known.at[len(reaches)], len(plane))
    band_copies = []
    for i, (m, p) in enumerate(shifts):
        target = along(m, turned(p))
        band_out[target[0]] = total_w[target[0]].astype(jnp.bfloat16)
        band_copies.append(
            send(band_out.at[target[0]], band_in.at[i], band_send, band_recv.at[i], target)
        )
    result = total_w[band]
    for i in reversed(range(len(shifts))):
        band_copies[i].wait_recv()
        result = result + band_in[i].astype(jnp.float32)
    final[mine, line] = (result * scale).astype(jnp.bfloat16)

    def pass_on(m, l, send_sem, recv_sem, target):
        piece = final.at[m, l]
        send(piece, piece, send_sem, recv_sem, target)

    def arrive(m, l):
        settle(final.at[m, l], gather_recv.at[m, l])

    def spread(l):
        for step in reversed(away_steps):
            pass_on(mine, l, across_send, gather_recv.at[mine, l], device(near(step, 1)))
        pass_on(mine, l, forward_send, forward_recv, partner)

    for m in masks:
        pass_on(mine, line, along_send, gather_recv.at[mine, line], along(m, pair))
    order = [0] + masks[::-1]
    spread(line)
    settle(band_out.at[: total - 1], band_send)
    settle(grads.at[: samples - 1], grads_send)
    settle(rows_all.at[: len(side_steps) + 1], rows_send)
    if side_steps:
        settle(rows_all.at[: len(side_steps)], rows_forward)
    for away, copy in row_copies:
        pl.when(away)(copy.wait_send)
    pl.when(not_first)(up_halo.wait_send)
    pl.when(not_last)(down_halo.wait_send)
    for m in order[1:]:
        arrive(mine, flip(line, m))
        spread(flip(line, m))
    settle(final.at[0, : lines - 1], along_send)
    for m in order:
        for step in away_steps:
            source = member(behind(step, 1))
            arrive(source, flip(line, m))
            pass_on(source, flip(line, m), forward_send, forward_recv, partner)
    settle(final.at[: len(away_steps)], across_send)
    settle(final.at[: len(away_steps) + 1], forward_send)
    settle(final.at[: len(away_steps) + 1], forward_recv)


def body(fields, embed_w, embed_b, merge_ids, ln_gain, w_up, w_down, d_out):
    bands = lax.axis_size("band")
    samples = lax.axis_size("sample")
    lon = merge_ids.shape[1]
    counts, starts = band_layout(bands, lon)
    shard_rows = starts[-1] // bands
    rotate = shard_rows - lon // 8
    granule = functools.reduce(math.gcd, counts + [rotate, shard_rows])
    features, model_width = embed_w.shape
    channels, lat_rows, cells = fields.shape[1:]
    pad_v = round_up(channels, 16)
    inner = 2 if bands <= 8 else 1
    lines, group = bands // inner, inner * samples
    part_rows = round_up(-(-(features + 1) // bands), 8)
    width = round_up(bands * part_rows, 128)
    vmem = pl.BlockSpec(memory_space=pltpu.VMEM)
    dma = pltpu.SemaphoreType.DMA

    scale = 1.0 / math.sqrt(samples * starts[-1])
    columns = model_width // samples
    hidden_width = w_up.shape[1]
    piece = (bands, part_rows, columns)
    bf16 = jnp.bfloat16
    hbm = pl.BlockSpec(memory_space=pl.ANY)
    f32 = jnp.float32
    mixed, final = pl.pallas_call(
        functools.partial(
            kernel, counts, rotate, shard_rows, features, granule, samples, inner, scale
        ),
        out_shape=(
            pltpu.VMEM((shard_rows, model_width), bf16),
            pltpu.VMEM((group, lines) + piece[1:], bf16),
        ),
        in_specs=[pl.BlockSpec(memory_space=pltpu.HBM)] * 8,
        out_specs=(vmem, vmem),
        scratch_shapes=[
            pltpu.VMEM(fields.shape[1:], bf16),
            pltpu.VMEM(merge_ids.shape, jnp.int32),
            pltpu.VMEM((1, model_width), f32),
            pltpu.VMEM((1, model_width), f32),
            pltpu.VMEM(embed_w.shape, bf16),
            pltpu.VMEM(w_up.shape, bf16),
            pltpu.VMEM(w_down.shape, bf16),
            pltpu.VMEM((shard_rows, model_width), bf16),
            pltpu.VMEM((4 * pad_v, cells), bf16),
            pltpu.VMEM((lon, width), bf16),
            pltpu.VMEM((samples, shard_rows, width), bf16),
            pltpu.VMEM((shard_rows, model_width), bf16),
            pltpu.VMEM((samples, shard_rows, columns), bf16),
            pltpu.VMEM((samples - 1, shard_rows, columns), bf16),
            pltpu.VMEM(piece, bf16),
            pltpu.VMEM((bands - 1,) + piece[1:], bf16),
            pltpu.VMEM(piece, f32),
            dma((8,)),
            dma((2,)),
            dma((2,)),
            dma((lon // granule,)),
            dma(()),
            dma(()),
            dma(()),
            dma((samples,)),
            dma(()),
            dma((samples - 1,)),
            dma(()),
            dma((bands - 1,)),
            dma(()),
            dma(()),
            dma(()),
            dma(()),
            dma((group, lines)),
            pltpu.VMEM((shard_rows, hidden_width), bf16),
            pltpu.VMEM((shard_rows, hidden_width), bf16),
            pltpu.VMEM((shard_rows, model_width), jnp.float32),
            pltpu.SemaphoreType.REGULAR(((bands - 1).bit_length(),)),
        ],
        compiler_params=pltpu.CompilerParams(
            collective_id=0, has_side_effects=True, vmem_limit_bytes=32 << 20
        ),
    )(*[
        pltpu.with_memory_space_constraint(x, pltpu.HBM)
        for x in (
            fields[0], merge_ids, embed_b[None], ln_gain[None], embed_w, w_up, w_down, d_out[0]
        )
    ])
    mixed, grad, grad_b = pl.pallas_call(
        functools.partial(emit, inner),
        out_shape=(
            jax.ShapeDtypeStruct((shard_rows, model_width), bf16),
            jax.ShapeDtypeStruct((features, model_width), f32),
            jax.ShapeDtypeStruct((1, model_width), f32),
        ),
        in_specs=[vmem, vmem],
        out_specs=(hbm, hbm, hbm),
        scratch_shapes=[
            pltpu.VMEM((features, model_width), f32),
            pltpu.VMEM((1, model_width), f32),
            dma((2 + lines,)),
        ],
        compiler_params=pltpu.CompilerParams(vmem_limit_bytes=16 << 20),
    )(mixed, final)
    return mixed[None], grad, grad_b[0]


def solution(mesh):
    return jax.shard_map(
        body,
        mesh=mesh,
        in_specs=(
            P("sample", None, "band", None),
            P(),
            P(),
            P("band", None),
            P(),
            P(),
            P(),
            P("sample", "band", None),
        ),
        out_specs=(P("sample", "band", None), P(), P()),
        check_vma=False,
    )
```

```python
import functools
import math

import jax
import jax.numpy as jnp
from jax import lax
from jax.experimental import pallas as pl
from jax.experimental.pallas import tpu as pltpu
from jax.sharding import PartitionSpec as P

MESH = pl.DeviceIdType.MESH


def round_up(value, step):
    return -(-value // step) * step


def band_layout(band_total, lon_patches):
    counts = []
    for b in range(band_total):
        distance = min(b, band_total - 1 - b)
        factor = 4 if distance < band_total // 8 else 2 if distance < band_total // 4 else 1
        counts.append(lon_patches // factor)
    starts = [0]
    for c in counts:
        starts.append(starts[-1] + c)
    return (counts, starts)


def flip(value, mask):
    for bit in range(mask.bit_length()):
        if mask >> bit & 1:
            value = value + (1 - 2 * lax.rem(lax.div(value, 1 << bit), 2)) * (1 << bit)
    return value


def emit(inner, mixed_ref, final_ref, mixed_out, w_out, b_out, staged, b_staged, sems):
    members, lines, part_rows, columns = final_ref.shape
    blocks = members // inner
    features = w_out.shape[0]
    copies = [pltpu.make_async_copy(mixed_ref, mixed_out, sems.at[0])]
    copies[0].start()
    for line in range(lines):
        start = line * inner * part_rows
        for pair in range(inner):
            low = start + pair * part_rows
            rows = min(part_rows, features - low)
            for m in range(blocks):
                values = final_ref[pair * blocks + m, line].astype(jnp.float32)
                if rows > 0:
                    staged[low : low + rows, m * columns : (m + 1) * columns] = values[:rows]
                if low <= features < low + part_rows:
                    b_staged[:, m * columns : (m + 1) * columns] = values[
                        features - low : features - low + 1
                    ]
        rows = min(inner * part_rows, features - start)
        if rows > 0:
            span = pl.ds(start, rows)
            copy = pltpu.make_async_copy(staged.at[span], w_out.at[span], sems.at[2 + line])
            copy.start()
            copies.append(copy)
    copies.append(pltpu.make_async_copy(b_staged, b_out, sems.at[1]))
    copies[-1].start()
    for copy in copies:
        copy.wait()


def kernel(
    counts, rotate, shard_rows, features, granule, samples, inner, scale,
    own_hbm, ids_hbm, bias_hbm, gain_hbm, embed_hbm, up_hbm, down_hbm, cot_hbm,
    mixed_ref, final,
    own_ref, ids_ref, bias_ref, gain_ref,
    embed, up, down, cot, grid, packed, rows_all, normed, grads, grads_in,
    band_out, band_in, total_w,
    load, halo_send, halo_recv, row_send, row_recv,
    rows_send, rows_forward, rows_done, grads_send, grads_recv,
    band_send, band_recv, along_send, across_send, forward_send, forward_recv, gather_recv,
    d_hid, hid, held_tokens, known,
):
    total = len(counts)
    lines, chips = total // inner, samples // 2
    band, sample = lax.axis_index("band"), lax.axis_index("sample")
    line, pair = lax.div(band, inner), lax.rem(band, inner)
    chip, core = lax.div(sample, 2), lax.rem(sample, 2)
    half = lax.div(line, lines // 2)
    other = 1 - core
    partner = (band, 2 * chip + other)

    def near(step, turn):
        p, c = step
        return (lax.rem(pair + p, inner), lax.rem(chip + c, chips), core if turn == 0 else other)

    def behind(step, turn):
        p, c = step
        return (
            lax.rem(pair + inner - p, inner),
            lax.rem(chip + chips - c, chips),
            core if turn == 0 else other,
        )

    def device(spot):
        p, c, k = spot
        return (line * inner + p, 2 * c + k)

    def block(spot):
        p, c, k = spot
        return 2 * c + lax.rem(k + half, 2)

    def member(spot):
        return spot[0] * samples + block(spot)

    steps = [(p, c) for p in range(inner) for c in range(chips)]
    away_steps = sorted(steps[1:], key=lambda step: (step[0] > 0) + (step[1] > 0))
    here_spot = (pair, chip, core)
    my_block, mine = block(here_spot), member(here_spot)
    side_steps = [step for step in away_steps if step[0] == 0]
    peer_keys = [((0, 0), 1)] + [(step, turn) for step in side_steps for turn in (1, 0)]
    masks = sorted(range(1, lines), reverse=True)

    def along(mask, p):
        return (flip(line, mask) * inner + p, 2 * chip + (other if 2 * mask >= lines else core))

    shifts = [(mask, p) for mask in masks for p in reversed(range(inner))]
    shifts += [(0, p) for p in range(1, inner)]

    def turned(p):
        return lax.rem(pair + p, inner)


    def beside(reach):
        return [(lax.rem(band + o, total), sample) for o in {reach, total - reach}]

    def say(i, devices):
        for target in devices:
            pl.semaphore_signal(known.at[i], inc=1, device_id=target, device_id_type=MESH)

    plane = [partner] + [device(near(step, turn)) for step in side_steps for turn in (0, 1)]
    reaches = [1 << i for i in range((total - 1).bit_length() - 1)]
    greeted = beside(1) + plane
    barrier = pltpu.get_barrier_semaphore()
    for peer in greeted:
        pl.semaphore_signal(barrier, inc=1, device_id=peer, device_id_type=MESH)

    loads = [
        pltpu.make_async_copy(src, dst, load.at[i])
        for i, (src, dst) in enumerate(
            (
                (embed_hbm, embed), (up_hbm, up), (down_hbm, down), (cot_hbm, cot),
                (own_hbm, own_ref), (ids_hbm, ids_ref), (bias_hbm, bias_ref), (gain_hbm, gain_ref),
            )
        )
    ]
    for i in (4, 5, 3, 2, 0, 6, 7, 1):
        loads[i].start()
    def remote(src, dst, send, recv, device):
        return pltpu.make_async_remote_copy(
            src_ref=src, dst_ref=dst, send_sem=send, recv_sem=recv,
            device_id=device, device_id_type=MESH,
        )

    pad_v = grid.shape[0] // 4
    landed = rows_all.at[sample]
    up_halo = remote(
        grid.at[pl.ds(0, pad_v)], grid.at[pl.ds(3 * pad_v, pad_v)],
        halo_send.at[0], halo_recv.at[0], (lax.rem(band + total - 1, total), sample),
    )
    down_halo = remote(
        grid.at[pl.ds(pad_v, pad_v)], grid.at[pl.ds(2 * pad_v, pad_v)],
        halo_send.at[1], halo_recv.at[1], (lax.rem(band + 1, total), sample),
    )
    is_first, is_last = band == 0, band == total - 1
    not_first, not_last = band > 0, band < total - 1
    channels = own_ref.shape[0]
    loads[4].wait()
    grid[pl.ds(0, 2 * pad_v), :] = jnp.zeros((2 * pad_v, grid.shape[1]), grid.dtype)
    for r in range(2):
        grid[pl.ds(r * pad_v, channels), :] = own_ref[:, r, :]
    lon, cells, width = packed.shape[0], grid.shape[1], packed.shape[1]
    slot = lax.broadcasted_iota(jnp.int32, (lon, lon), 0)
    loads[5].wait()
    onehot = (ids_ref[...] == slot).astype(jnp.float32)
    members = jnp.sum(onehot, axis=1, keepdims=True)
    safe = jnp.where(members > 0, members, 1.0)
    onehot = onehot.astype(jnp.bfloat16)
    patch = lax.broadcasted_iota(jnp.int32, (lon, cells), 0)
    cell = lax.broadcasted_iota(jnp.int32, (lon, cells), 1)
    picks = [
        jnp.dot(
            onehot, (cell == 2 * patch + q).astype(jnp.float32).astype(jnp.bfloat16),
            preferred_element_type=jnp.float32,
        ).astype(jnp.bfloat16)
        for q in range(2)
    ]
    rows = lax.broadcasted_iota(jnp.int32, (2 * pad_v, width), 0)
    column = lax.broadcasted_iota(jnp.int32, (2 * pad_v, width), 1)
    second = (rows >= pad_v).astype(jnp.int32)
    place = 8 * (rows - pad_v * second)

    def moves(first, step, q):
        return (column == place + 2 * (first + step * second) + q).astype(jnp.float32).astype(
            jnp.bfloat16
        )

    own_moves = [moves(1, 1, q) for q in range(2)]
    halo_moves = [moves(0, 3, q) for q in range(2)]
    picks = jnp.concatenate(picks, axis=0)

    def pooled(low, turns):
        summed = lax.dot_general(
            picks, grid[pl.ds(low, 2 * pad_v), :], (((1,), (1,)), ((), ())),
            preferred_element_type=jnp.float32,
        )
        return sum(
            jnp.dot(
                (summed[q * lon : (q + 1) * lon] / safe).astype(jnp.bfloat16), turns[q],
                preferred_element_type=jnp.float32,
            )
            for q in range(2)
        )

    pl.semaphore_wait(barrier, len(greeted))
    say(0, beside(1))
    pl.when(not_first)(up_halo.start)
    pl.when(not_last)(down_halo.start)

    @pl.when(is_first)
    def _():
        grid[pl.ds(2 * pad_v, pad_v), :] = jnp.zeros((pad_v, grid.shape[1]), grid.dtype)

    @pl.when(is_last)
    def _():
        grid[pl.ds(3 * pad_v, pad_v), :] = jnp.zeros((pad_v, grid.shape[1]), grid.dtype)

    ordered = pooled(0, own_moves)
    pl.when(not_last)(up_halo.wait_recv)
    pl.when(not_first)(down_halo.wait_recv)
    ordered = ordered + pooled(2 * pad_v, halo_moves)
    ones = lax.broadcasted_iota(jnp.int32, (lon, width), 1) == features
    packed[...] = jnp.where(ones, 1.0, ordered).astype(packed.dtype)

    pl.semaphore_wait(known.at[0], len(beside(1)))
    say(1, beside(2))
    my_count = sum(jnp.where(band == b, c, 0) for b, c in enumerate(counts))
    my_start = rotate + sum(jnp.where(band > b, c, 0) for b, c in enumerate(counts))
    row_copies = []
    for i in range(lon // granule):
        unwrapped = my_start + granule * i
        target = lax.rem(lax.div(unwrapped, shard_rows), total)
        offset = pl.multiple_of(lax.rem(unwrapped, shard_rows), granule)
        valid = granule * i < my_count
        here = target == band
        src, dst = packed.at[pl.ds(granule * i, granule)], landed.at[pl.ds(offset, granule)]
        copy = remote(src, dst, row_send.at[i], row_recv, (target, sample))
        keep = pltpu.make_async_copy(src, dst, row_recv)
        away = jnp.logical_and(valid, jnp.logical_not(here))
        pl.when(away)(copy.start)
        pl.when(jnp.logical_and(valid, here))(keep.start)
        row_copies.append((away, copy))
    for i in (2, 3):
        loads[i].wait()
    hidden_width = up.shape[1]
    tile = 512
    across = (((1,), (1,)), ((), ()))
    for t in range(hidden_width // tile):
        span = slice(t * tile, (t + 1) * tile)
        d_hid[:, span] = lax.dot_general(
            cot[...], down[span, :], across, preferred_element_type=jnp.float32
        ).astype(jnp.bfloat16)
    for i, reach in enumerate(reaches[1:]):
        pl.semaphore_wait(known.at[i + 1], len(beside(reach)))
        say(i + 2, beside(2 * reach) if 2 * reach in reaches else plane)
    pltpu.make_async_copy(landed, landed, row_recv).wait()

    def send(src, dst, send_sem, recv_sem, target):
        copy = remote(src, dst, send_sem, recv_sem, target)
        copy.start()
        return copy

    def settle(ref, semaphore):
        pltpu.make_async_copy(ref, ref, semaphore).wait()

    def send_rows(m, send_sem, target):
        send(rows_all.at[m], rows_all.at[m], send_sem, rows_done.at[m], target)

    def rows_arrive(m):
        pltpu.make_async_copy(rows_all.at[m], rows_all.at[m], rows_done.at[m]).wait()

    for step in side_steps:
        send_rows(sample, rows_send, device(near(step, 1)))
    send_rows(sample, rows_send, partner)

    for i in (0, 6, 7):
        loads[i].wait()
    tokens = (
        jnp.dot(landed[:, :features], embed[...], preferred_element_type=jnp.float32)
        + bias_ref[...]
    ).astype(jnp.bfloat16).astype(jnp.float32)
    model_width = tokens.shape[1]
    centred = tokens - jnp.mean(tokens, axis=-1, keepdims=True)
    inverse = lax.rsqrt(jnp.mean(centred * centred, axis=-1, keepdims=True) + 1e-05)
    normed[...] = (centred * inverse * gain_ref[...]).astype(jnp.bfloat16)
    held_tokens[...] = tokens
    d_normed = jnp.zeros_like(tokens)
    loads[1].wait()
    slope = math.sqrt(2.0 / math.pi)
    for t in range(hidden_width // tile):
        span = slice(t * tile, (t + 1) * tile)
        pre = jnp.dot(normed[...], up[:, span], preferred_element_type=jnp.float32)
        d_hidden = d_hid[:, span].astype(jnp.float32)
        bend = (slope * 0.044715) * (pre * pre)
        inner_arg = pre * (bend + slope)
        bent = jnp.tanh(inner_arg)
        cdf = 0.5 * bent + 0.5
        hid[:, span] = (pre * cdf).astype(jnp.bfloat16)
        steep = cdf * ((1.0 - bent) * (inner_arg + (pre + pre) * bend) + 1.0)
        d_pre = (d_hidden * steep).astype(jnp.bfloat16)
        d_normed = d_normed + lax.dot_general(
            d_pre, up[:, span], across, preferred_element_type=jnp.float32
        )
    d_scaled = d_normed.astype(jnp.bfloat16).astype(jnp.float32) * gain_ref[...]
    pull = jnp.sum(d_scaled * centred, axis=-1, keepdims=True) * (
        inverse * inverse * inverse / model_width
    )
    drift = jnp.mean(d_scaled, axis=-1, keepdims=True) * inverse
    d_tokens = d_scaled * inverse - centred * pull - drift
    grad = (cot[...].astype(jnp.float32) + d_tokens).astype(jnp.bfloat16)
    columns = grads.shape[2]
    for m in range(samples):
        grads[m] = grad[:, m * columns : (m + 1) * columns]

    grad_copies = {}
    for i, key in reversed(list(enumerate(peer_keys))):
        spot = near(*key)
        grad_copies[key] = send(
            grads.at[block(spot)], grads_in.at[i], grads_send, grads_recv.at[i],
            device(spot),
        )

    mixed = held_tokens[...]
    for t in range(hidden_width // tile):
        span = slice(t * tile, (t + 1) * tile)
        mixed = mixed + jnp.dot(hid[:, span], down[span, :], preferred_element_type=jnp.float32)
    mixed_ref[...] = mixed.astype(jnp.bfloat16)
    part_rows = total_w.shape[1]
    span_rows = total * part_rows

    def product(s, values):
        full = lax.dot_general(
            rows_all[s], values, (((0,), (0,)), ((), ())), preferred_element_type=jnp.float32
        )
        return full[:span_rows].reshape(total, part_rows, columns)

    def origin(key):
        return device(behind(*key))[1]

    def add_product(key):
        grad_copies[key].wait_recv()
        total_w[...] += product(origin(key), grads_in[peer_keys.index(key)])

    total_w[...] = product(sample, grads[my_block])
    rows_arrive(origin(((0, 0), 1)))
    add_product(((0, 0), 1))
    for i, step in enumerate(side_steps):
        source = origin((step, 1))
        rows_arrive(source)
        send_rows(source, rows_forward, partner)
        add_product((step, 1))
    for step in side_steps:
        rows_arrive(origin((step, 0)))
        add_product((step, 0))

    pl.semaphore_wait(known.at[len(reaches)], len(plane))
    band_copies = []
    for i, (m, p) in enumerate(shifts):
        target = along(m, turned(p))
        band_out[target[0]] = total_w[target[0]].astype(jnp.bfloat16)
        band_copies.append(
            send(band_out.at[target[0]], band_in.at[i], band_send, band_recv.at[i], target)
        )
    result = total_w[band]
    for i in reversed(range(len(shifts))):
        band_copies[i].wait_recv()
        result = result + band_in[i].astype(jnp.float32)
    final[mine, line] = (result * scale).astype(jnp.bfloat16)

    def pass_on(m, l, send_sem, recv_sem, target):
        piece = final.at[m, l]
        send(piece, piece, send_sem, recv_sem, target)

    def arrive(m, l):
        settle(final.at[m, l], gather_recv.at[m, l])

    def spread(l):
        for step in reversed(away_steps):
            pass_on(mine, l, across_send, gather_recv.at[mine, l], device(near(step, 1)))
        pass_on(mine, l, forward_send, forward_recv, partner)

    for m in masks:
        pass_on(mine, line, along_send, gather_recv.at[mine, line], along(m, pair))
    order = [0] + masks[::-1]
    spread(line)
    settle(band_out.at[: total - 1], band_send)
    settle(grads.at[: samples - 1], grads_send)
    settle(rows_all.at[: len(side_steps) + 1], rows_send)
    if side_steps:
        settle(rows_all.at[: len(side_steps)], rows_forward)
    for away, copy in row_copies:
        pl.when(away)(copy.wait_send)
    pl.when(not_first)(up_halo.wait_send)
    pl.when(not_last)(down_halo.wait_send)
    for m in order[1:]:
        arrive(mine, flip(line, m))
        spread(flip(line, m))
    settle(final.at[0, : lines - 1], along_send)
    for m in order:
        for step in away_steps:
            source = member(behind(step, 1))
            arrive(source, flip(line, m))
            pass_on(source, flip(line, m), forward_send, forward_recv, partner)
    settle(final.at[: len(away_steps)], across_send)
    settle(final.at[: len(away_steps) + 1], forward_send)
    settle(final.at[: len(away_steps) + 1], forward_recv)


def body(fields, embed_w, embed_b, merge_ids, ln_gain, w_up, w_down, d_out):
    bands = lax.axis_size("band")
    samples = lax.axis_size("sample")
    lon = merge_ids.shape[1]
    counts, starts = band_layout(bands, lon)
    shard_rows = starts[-1] // bands
    rotate = shard_rows - lon // 8
    granule = functools.reduce(math.gcd, counts + [rotate, shard_rows])
    features, model_width = embed_w.shape
    channels, lat_rows, cells = fields.shape[1:]
    pad_v = round_up(channels, 16)
    inner = 2 if bands <= 8 else 1
    lines, group = bands // inner, inner * samples
    part_rows = round_up(-(-(features + 1) // bands), 8)
    width = round_up(bands * part_rows, 128)
    vmem = pl.BlockSpec(memory_space=pltpu.VMEM)
    dma = pltpu.SemaphoreType.DMA

    scale = 1.0 / math.sqrt(samples * starts[-1])
    columns = model_width // samples
    hidden_width = w_up.shape[1]
    piece = (bands, part_rows, columns)
    bf16 = jnp.bfloat16
    hbm = pl.BlockSpec(memory_space=pl.ANY)
    f32 = jnp.float32
    mixed, final = pl.pallas_call(
        functools.partial(
            kernel, counts, rotate, shard_rows, features, granule, samples, inner, scale
        ),
        out_shape=(
            pltpu.VMEM((shard_rows, model_width), bf16),
            pltpu.VMEM((group, lines) + piece[1:], bf16),
        ),
        in_specs=[pl.BlockSpec(memory_space=pltpu.HBM)] * 8,
        out_specs=(vmem, vmem),
        scratch_shapes=[
            pltpu.VMEM(fields.shape[1:], bf16),
            pltpu.VMEM(merge_ids.shape, jnp.int32),
            pltpu.VMEM((1, model_width), f32),
            pltpu.VMEM((1, model_width), f32),
            pltpu.VMEM(embed_w.shape, bf16),
            pltpu.VMEM(w_up.shape, bf16),
            pltpu.VMEM(w_down.shape, bf16),
            pltpu.VMEM((shard_rows, model_width), bf16),
            pltpu.VMEM((4 * pad_v, cells), bf16),
            pltpu.VMEM((lon, width), bf16),
            pltpu.VMEM((samples, shard_rows, width), bf16),
            pltpu.VMEM((shard_rows, model_width), bf16),
            pltpu.VMEM((samples, shard_rows, columns), bf16),
            pltpu.VMEM((samples - 1, shard_rows, columns), bf16),
            pltpu.VMEM(piece, bf16),
            pltpu.VMEM((bands - 1,) + piece[1:], bf16),
            pltpu.VMEM(piece, f32),
            dma((8,)),
            dma((2,)),
            dma((2,)),
            dma((lon // granule,)),
            dma(()),
            dma(()),
            dma(()),
            dma((samples,)),
            dma(()),
            dma((samples - 1,)),
            dma(()),
            dma((bands - 1,)),
            dma(()),
            dma(()),
            dma(()),
            dma(()),
            dma((group, lines)),
            pltpu.VMEM((shard_rows, hidden_width), bf16),
            pltpu.VMEM((shard_rows, hidden_width), bf16),
            pltpu.VMEM((shard_rows, model_width), jnp.float32),
            pltpu.SemaphoreType.REGULAR(((bands - 1).bit_length(),)),
        ],
        compiler_params=pltpu.CompilerParams(
            collective_id=0, has_side_effects=True, vmem_limit_bytes=32 << 20
        ),
    )(*[
        pltpu.with_memory_space_constraint(x, pltpu.HBM)
        for x in (
            fields[0], merge_ids, embed_b[None], ln_gain[None], embed_w, w_up, w_down, d_out[0]
        )
    ])
    mixed, grad, grad_b = pl.pallas_call(
        functools.partial(emit, inner),
        out_shape=(
            jax.ShapeDtypeStruct((shard_rows, model_width), bf16),
            jax.ShapeDtypeStruct((features, model_width), f32),
            jax.ShapeDtypeStruct((1, model_width), f32),
        ),
        in_specs=[vmem, vmem],
        out_specs=(hbm, hbm, hbm),
        scratch_shapes=[
            pltpu.VMEM((features, model_width), f32),
            pltpu.VMEM((1, model_width), f32),
            dma((2 + lines,)),
        ],
        compiler_params=pltpu.CompilerParams(vmem_limit_bytes=16 << 20),
    )(mixed, final)
    return mixed[None], grad, grad_b[0]


def solution(mesh):
    return jax.shard_map(
        body,
        mesh=mesh,
        in_specs=(
            P("sample", None, "band", None),
            P(),
            P(),
            P("band", None),
            P(),
            P(),
            P(),
            P("sample", "band", None),
        ),
        out_specs=(P("sample", "band", None), P(), P()),
        check_vma=False,
    )
```
